512 devices in a mesh: span: 64 (over z_lo, x, core), chord: 8 (over z_hi, y).
Axes of the slice: x: 4, y: 4, z: 16 (z_hi: 2, z_lo: 8; z = z_hi * 8 + z_lo), core: 2. Of those that a mesh axis runs over, the one named last changes fastest.
Arguments:
- adjoint_flow: float32 [5, 16, 512, 1024], P(None, None, 'span', 'chord'), may hold values from -6 to 6
- flow_grad: float32 [5, 16, 512, 1024], P(None, None, 'span', 'chord'), may hold values from -6 to 6
- diagonal: float32 [16, 512, 1024], P(None, 'span', 'chord'), may hold values from 4 to 6
- couplings: float32 [3, 16, 512, 1024], P(None, None, 'span', 'chord'), may hold values from 0.3 to 1.5
- upwind: float32 [3, 5, 5], replicated, may hold values from -2.5 to 2.5
- downwind: float32 [3, 5, 5], replicated, may hold values from -2.5 to 2.5
- pressure_row: float32 [5], replicated, may hold values from -4 to 4
- face_normal: float32 [3, 512, 1024], P(None, 'span', 'chord'), may hold values from -6 to 6
- face_node: int32 [512, 1024], P('span', 'chord'), may hold values from 0 to 65535, as said below
- face_count: int32 [64, 8], P('span', 'chord'), may hold values from 128 to 1024, as said below
- adjoint_shell: float32 [6, 65536], P(None, 'span'), may hold values from -6 to 6
- shell_grad: float32 [6, 65536], P(None, 'span'), may hold values from -6 to 6
- node_precond: float32 [6, 6, 65536], P(None, None, 'span'), as said below
- element_stiffness: float32 [24, 24, 65536], P(None, None, ('span', 'chord')), as said below
- connectivity: int32 [4, 65536], P(None, ('span', 'chord')), may hold values from 0 to 65535, as said below
Outputs:
- flow_adjoint: float32 [5, 16, 512, 1024], P(None, None, 'span', 'chord')
- shell_adjoint: float32 [6, 65536], P(None, 'span')
The draws below stay inside these ranges and needn't reach their ends.
Inputs may be any that keep to these rules, and one draw needn't show every extreme that they name: `face_node`: a wall face in the span cells of span index s names a node from max(s - 1, 0) * 1024 to min(s + 2, 64) * 1024 - 1. `face_count`: on each device the wall faces in use are the first ones in span-major, chord-minor order. `connectivity`: the elements of span index s use nodes from s * 1024 to min((s + 1) * 1024 + 64, 65536) - 1. `node_precond`: each node block is near 0.15 times the identity. `element_stiffness`: each element block is symmetric and near the identity.
All inputs are finite; a program needn't handle non-finite values.
Results may differ from the reference program's by a relative error of at most 0.00013.
Values sent between devices are 32-bit elements; how exact they have to be, the bound alone decides.
No kernel may reach another device: no remote copies, remote signals or barrier semaphores. Data moves between devices by JAX's collectives and lax.ppermute only.
A program may use at most 64 MiB of HBM per device.

```python
import math
import jax
import jax.numpy as jnp
from jax import lax

CN = 16
CS = 8
CC = 128
NODE_DEV = 1024
ELEM_DEV = 128
NB = 64
SW = 4
SS = 3
NS = 512
NC = 1024
NODES = 65536
ELEMS = 65536
WALLF = 1024


def draw_face_node(key, part):
    span_rows = jnp.arange(NS, dtype=jnp.int32)[:, None]
    owner = span_rows // CS
    lower = jnp.maximum(owner - 1, 0) * NODE_DEV
    upper = jnp.minimum(owner + 2, NS // CS) * NODE_DEV
    raw_bits = jax.random.randint(key, (NS, NC), 0, 1 << 24)
    nodes = lower + raw_bits % (upper - lower)
    leading = span_rows % CS == 0
    local_chord = jnp.arange(NC, dtype=jnp.int32)[None, :] % CC
    nodes = jnp.where(leading & (local_chord == 0), lower, nodes)
    nodes = jnp.where(leading & (local_chord == 1), upper - 1, nodes)
    return nodes.astype(jnp.int32)


def draw_face_count(key, part):
    spans = NS // CS
    chords = NC // CC
    counts = jax.random.randint(key, (spans, chords), WALLF // 8, WALLF + 1)
    picked = jax.random.randint(jax.random.fold_in(key, 11), (spans, 1), 0, chords)
    chord_ids = jnp.arange(chords, dtype=jnp.int32)[None, :]
    counts = jnp.where(chord_ids == picked, WALLF, counts)
    counts = jnp.where(chord_ids == (picked + 1) % chords, WALLF // 8, counts)
    return counts.astype(jnp.int32)


def draw_connectivity(key, part):
    owners = NODES // NODE_DEV
    element = jnp.arange(ELEMS, dtype=jnp.int32)[None, :]
    owner = element // (ELEMS // owners)
    lower = owner * NODE_DEV
    upper = jnp.minimum(lower + NODE_DEV + NB, NODES)
    raw_bits = jax.random.randint(key, (4, ELEMS), 0, 1 << 24)
    nodes = lower + raw_bits % (upper - lower)
    leading = element % ELEM_DEV == 0
    corner = jnp.arange(4, dtype=jnp.int32)[:, None]
    nodes = jnp.where(leading & (corner == 0), lower, nodes)
    nodes = jnp.where(leading & (corner == 1), upper - 1, nodes)
    return nodes.astype(jnp.int32)


def draw_element_stiffness(key, part):
    noise = jax.random.normal(key, (24, 24, ELEMS), jnp.float32)
    symmetric = 0.5 * (noise + jnp.transpose(noise, (1, 0, 2)))
    identity = jnp.eye(24, dtype=jnp.float32)[:, :, None]
    return (identity + 0.06 * symmetric).astype(jnp.float32)


def draw_node_precond(key, part):
    noise = jax.random.normal(key, (6, 6, NODES), jnp.float32)
    identity = jnp.eye(6, dtype=jnp.float32)[:, :, None]
    return (0.15 * identity + 0.02 * noise).astype(jnp.float32)


def block_scale(stream_key, shape, pieces, low, high):
    def one(position, shards_of):
        draws = jax.random.uniform(jax.random.fold_in(jax.random.fold_in(stream_key, 6), position), (shards_of,), jnp.float32, low / len(pieces), high / len(pieces))
        return jnp.repeat(jnp.exp(draws), shape[position] // shards_of).reshape((-1,) + (1,) * (len(shape) - position - 1))

    level = one(*pieces[0])
    for cut in pieces[1:]:
        level = level * one(*cut)
    return level


def gaussian(key, dims, scale, most, shards=(), kind=jnp.bfloat16):
    entries = jax.random.normal(key, dims, jnp.float32) * scale
    if len(shards) > 0:
        entries = block_scale(key, dims, shards, -0.22, 0.18) * entries
    return jnp.clip(entries, min=-most, max=most).astype(kind)


def setup_inputs(seed: int = 0) -> dict:
    keys = jax.random.split(jax.random.key(seed), 16)
    return {
        "adjoint_flow": gaussian(keys[0], (5, CN, NS, NC), 1.0, 6.0, ((2, 64), (3, 8)), jnp.float32),
        "flow_grad": gaussian(keys[1], (5, CN, NS, NC), 1.0, 6.0, ((2, 64), (3, 8)), jnp.float32),
        "diagonal": jnp.clip(4.0 + 2.0 * jax.random.uniform(keys[2], (CN, NS, NC), jnp.float32) ** block_scale(keys[2], (CN, NS, NC), ((1, 64), (2, 8)), -0.2, 0.2), 4.0, 6.0),
        "couplings": jnp.clip(jnp.exp(math.log(1.5) - 1.60943787 * jax.random.uniform(keys[3], (3, CN, NS, NC), jnp.float32) ** block_scale(keys[3], (3, CN, NS, NC), ((2, 64), (3, 8)), -0.2, 0.2)), 0.3, 1.5),
        "upwind": gaussian(keys[4], (3, 5, 5), 5 ** -0.5, 2.5, (), jnp.float32),
        "downwind": gaussian(keys[5], (3, 5, 5), 5 ** -0.5, 2.5, (), jnp.float32),
        "pressure_row": gaussian(keys[6], (5,), 1.0, 4.0, (), jnp.float32),
        "face_normal": gaussian(keys[7], (3, NS, NC), 1.0, 6.0, ((1, 64), (2, 8)), jnp.float32),
        "face_node": draw_face_node(jax.random.fold_in(keys[15], 71), 0),
        "face_count": draw_face_count(jax.random.fold_in(keys[15], 71), 0),
        "adjoint_shell": gaussian(keys[10], (6, NODES), 1.0, 6.0, ((1, 64),), jnp.float32),
        "shell_grad": gaussian(keys[11], (6, NODES), 1.0, 6.0, ((1, 64),), jnp.float32),
        "node_precond": draw_node_precond(jax.random.fold_in(keys[15], 71), 0),
        "element_stiffness": draw_element_stiffness(jax.random.fold_in(keys[15], 71), 0),
        "connectivity": draw_connectivity(jax.random.fold_in(keys[15], 71), 0),
    }


def relax_cells(state, inv_diag, couplings, source, upwind, downwind):
    centre = state[:, :, 1:-1, 1:-1]
    normal_pad = jnp.pad(centre, ((0, 0), (1, 1), (0, 0), (0, 0)))
    pairs = ((normal_pad[:, 2:], normal_pad[:, :-2]),
             (state[:, :, 2:, 1:-1], state[:, :, :-2, 1:-1]),
             (state[:, :, 1:-1, 2:], state[:, :, 1:-1, :-2]))
    neighbours = jnp.zeros_like(source)
    for direction in range(3):
        forward, backward = pairs[direction]
        flux_term = jnp.einsum("ij,jnsc->insc", upwind[direction], forward, precision=lax.Precision.HIGHEST)
        flux_term = flux_term + jnp.einsum("ij,jnsc->insc", downwind[direction], backward, precision=lax.Precision.HIGHEST)
        neighbours = neighbours + couplings[direction][None] * flux_term
    return inv_diag[None] * (source + neighbours)


def stiffness(field, element_stiffness, connectivity):
    count_elems = connectivity.shape[1]
    element_values = field[:, connectivity]
    element_values = jnp.transpose(element_values, (1, 0, 2)).reshape(24, count_elems)
    element_forces = jnp.einsum("ije,je->ie", element_stiffness, element_values, precision=lax.Precision.HIGHEST)
    element_forces = jnp.transpose(element_forces.reshape(4, 6, count_elems), (1, 0, 2)).reshape(6, 4 * count_elems)
    return jax.ops.segment_sum(element_forces.T, connectivity.reshape(-1), field.shape[1]).T


def reference(adjoint_flow, flow_grad, diagonal, couplings, upwind, downwind, pressure_row, face_normal, face_node, face_count, adjoint_shell, shell_grad, node_precond, element_stiffness, connectivity):
    wall_layer = adjoint_flow[:, 0]
    span_index = jnp.arange(NS, dtype=jnp.int32)[:, None]
    chord_index = jnp.arange(NC, dtype=jnp.int32)[None, :]
    local_index = (span_index % CS) * CC + chord_index % CC
    counts = face_count[span_index // CS, chord_index // CC]
    active = (local_index < counts).astype(jnp.float32)
    pressure = jnp.einsum("j,jsc->sc", pressure_row, wall_layer, precision=lax.Precision.HIGHEST) * active
    loads_face = face_normal * pressure[None]
    node_load = jax.ops.segment_sum(loads_face.reshape(3, -1).T, face_node.reshape(-1), NODES).T
    load_full = jnp.concatenate([node_load, jnp.zeros((3, NODES), jnp.float32)], axis=0)
    shell_state = adjoint_shell
    for turn_index in range(SS):
        residual = shell_grad - load_full - stiffness(shell_state, element_stiffness, connectivity)
        shell_state = shell_state + jnp.einsum("ijn,jn->in", node_precond, residual, precision=lax.Precision.HIGHEST)
    picked = shell_state[:3][:, face_node]
    disp = jnp.einsum("isc,isc->sc", face_normal, picked, precision=lax.Precision.HIGHEST) * active
    source = flow_grad.at[:, 0].add(-pressure_row[:, None, None] * disp[None])
    inv_diag = 1.0 / diagonal
    state = adjoint_flow
    for turn_index in range(SW):
        padded = jnp.pad(state, ((0, 0), (0, 0), (1, 1), (1, 1)))
        state = relax_cells(padded, inv_diag, couplings, source, upwind, downwind)
    return state, shell_state
```

```python
import jax
import jax.numpy as jnp
from jax import lax
from jax.sharding import PartitionSpec as P

NB = 64
SW = 4
SS = 3


def shifted(value, axis, steps):
    count = lax.axis_size(axis)
    initial, last = (max(0, -steps), min(count, count - steps))
    return lax.ppermute(value, axis, [(source, source + steps) for source in range(initial, last)])


def with_halo(cells, sides, width):
    for axis, dim in sides:
        count = lax.axis_size(axis)
        ends = count - 1
        head = lax.slice_in_dim(cells, 0, width, axis=dim)
        tail = lax.slice_in_dim(cells, cells.shape[dim] - width, cells.shape[dim], axis=dim)
        cells = jnp.concatenate(
            [
                lax.ppermute(tail, axis, [(i, (i + 1) % count) for i in range(ends)]),
                cells,
                lax.ppermute(head, axis, [((i + 1) % count, i) for i in range(ends)]),
            ],
            axis=dim,
        )
    return cells


def relax_cells(state, inv_diag, couplings, source, upwind, downwind):
    centre = state[:, :, 1:-1, 1:-1]
    normal_pad = jnp.pad(centre, ((0, 0), (1, 1), (0, 0), (0, 0)))
    pairs = (
        (normal_pad[:, 2:], normal_pad[:, :-2]),
        (state[:, :, 2:, 1:-1], state[:, :, :-2, 1:-1]),
        (state[:, :, 1:-1, 2:], state[:, :, 1:-1, :-2]),
    )
    neighbours = jnp.zeros_like(source)
    for direction in range(3):
        forward, backward = pairs[direction]
        flux_term = jnp.einsum(
            "ij,jnsc->insc", upwind[direction], forward, precision=lax.Precision.HIGHEST
        )
        flux_term = flux_term + jnp.einsum(
            "ij,jnsc->insc", downwind[direction], backward, precision=lax.Precision.HIGHEST
        )
        neighbours = neighbours + couplings[direction][None] * flux_term
    return inv_diag[None] * (source + neighbours)


def chord_sum(value):
    shape = value.shape
    total = value.reshape(-1, 128)
    count = lax.axis_size("chord")
    for bit in (1, 2, 4):
        total = total + lax.ppermute(total, "chord", [(c, c ^ bit) for c in range(count)])
    return total.reshape(shape)


def spread(partial_value, node_dev):
    own_block = partial_value[:, node_dev : 2 * node_dev]
    from_lower = shifted(partial_value[:, 2 * node_dev :], "span", 1)
    from_upper = shifted(partial_value[:, :node_dev], "span", -1)
    return own_block + from_lower + from_upper


def element_terms(field, element_stiffness, local_nodes):
    node_dev = field.shape[1]
    count_elems = local_nodes.shape[1]
    rim_nodes = shifted(field[:, :NB], "span", -1)
    extended = jnp.concatenate([field, rim_nodes], axis=1)
    element_values = extended[:, local_nodes]
    element_values = jnp.transpose(element_values, (1, 0, 2)).reshape(24, count_elems)
    element_forces = jnp.einsum(
        "ije,je->ie", element_stiffness, element_values, precision=lax.Precision.HIGHEST
    )
    element_forces = jnp.transpose(element_forces.reshape(4, 6, count_elems), (1, 0, 2)).reshape(
        6, 4 * count_elems
    )
    assembled = jax.ops.segment_sum(element_forces.T, local_nodes.reshape(-1), node_dev + NB).T
    spill = shifted(assembled[:, node_dev:], "span", 1)
    return assembled[:, :node_dev].at[:, :NB].add(spill)


def per_device(
    adjoint_flow,
    flow_grad,
    diagonal,
    couplings,
    upwind,
    downwind,
    pressure_row,
    face_normal,
    face_node,
    face_count,
    adjoint_shell,
    shell_grad,
    node_precond,
    element_stiffness,
    connectivity,
):
    span_at = lax.axis_index("span")
    node_dev = adjoint_shell.shape[1]
    wall_layer = adjoint_flow[:, 0]
    span_cells = wall_layer.shape[1]
    chord_cells = wall_layer.shape[2]
    local_index = (
        jnp.arange(span_cells, dtype=jnp.int32)[:, None] * chord_cells
        + jnp.arange(chord_cells, dtype=jnp.int32)[None, :]
    )
    active = (local_index < face_count[0, 0]).astype(jnp.float32)
    pressure = (
        jnp.einsum("j,jsc->sc", pressure_row, wall_layer, precision=lax.Precision.HIGHEST) * active
    )
    loads_face = face_normal * pressure[None]
    reach_index = face_node - (span_at - 1) * node_dev
    partial_value = jax.ops.segment_sum(
        loads_face.reshape(3, -1).T, reach_index.reshape(-1), 3 * node_dev
    ).T
    node_load = spread(partial_value, node_dev)
    load_part = jnp.concatenate([node_load, jnp.zeros((3, node_dev), jnp.float32)], axis=0)
    local_nodes = connectivity - span_at * node_dev
    shell_state = adjoint_shell
    for turn_index in range(SS):
        local_forces = element_terms(shell_state, element_stiffness, local_nodes)
        if turn_index == 0:
            first_total = chord_sum(jnp.concatenate([local_forces, load_part[:3]], axis=0))
            stiff_total = first_total[:6]
            load_full = jnp.concatenate(
                [first_total[6:], jnp.zeros((3, node_dev), jnp.float32)], axis=0
            )
        else:
            stiff_total = chord_sum(local_forces)
        residual = shell_grad - load_full - stiff_total
        shell_state = shell_state + jnp.einsum(
            "ijn,jn->in", node_precond, residual, precision=lax.Precision.HIGHEST
        )
    reach = with_halo(shell_state[:3], (("span", 1),), node_dev)
    picked = reach[:, reach_index]
    disp = jnp.einsum("isc,isc->sc", face_normal, picked, precision=lax.Precision.HIGHEST) * active
    source = flow_grad.at[:, 0].add(-pressure_row[:, None, None] * disp[None])
    inv_diag = 1.0 / diagonal
    state = adjoint_flow
    for turn_index in range(SW):
        padded = with_halo(state, (("span", 2), ("chord", 3)), 1)
        state = relax_cells(padded, inv_diag, couplings, source, upwind, downwind)
    return (state, shell_state)


def solution(mesh):
    return jax.shard_map(
        per_device,
        mesh=mesh,
        in_specs=(
            P(None, None, "span", "chord"),
            P(None, None, "span", "chord"),
            P(None, "span", "chord"),
            P(None, None, "span", "chord"),
            P(),
            P(),
            P(),
            P(None, "span", "chord"),
            P("span", "chord"),
            P("span", "chord"),
            P(None, "span"),
            P(None, "span"),
            P(None, None, "span"),
            P(None, None, ("span", "chord")),
            P(None, ("span", "chord")),
        ),
        out_specs=(P(None, None, "span", "chord"), P(None, "span")),
        check_vma=False,
    )
```

```python
import functools

import jax
import jax.numpy as jnp
from jax import lax
from jax.experimental import pallas as pl
from jax.experimental.pallas import tpu as pltpu
from jax.sharding import Mesh
from jax.sharding import PartitionSpec as P


F32 = jnp.float32
BF16 = jnp.bfloat16
NB = 64
SW = 4
LAYERS = 16
NODE_DEV = 1024
TILES = 9
EXT = TILES * 128
PLANES = 228
HALF = PLANES // 2
FIELDS = 15
SLOTS = 2 * PLANES
WIDTH = 4
PACKED = 49
BLOCKS = ((0, 0), (1, 0), (1, 1), (2, 0), (2, 1), (2, 2))
VM = pl.BlockSpec(memory_space=pltpu.VMEM)
SM = pl.BlockSpec(memory_space=pltpu.SMEM)
PARAMS = pltpu.CompilerParams(vmem_limit_bytes=48 << 20)


def call(body, out, ins, specs, flops, scratch=(), aliases=None):
    return pl.pallas_call(
        body,
        out_shape=out,
        in_specs=specs,
        out_specs=jax.tree.map(lambda _: VM, out),
        scratch_shapes=list(scratch),
        input_output_aliases=aliases or {},
        compiler_params=PARAMS,
        cost_estimate=pl.CostEstimate(flops=flops, bytes_accessed=flops // 8, transcendentals=0),
    )(*ins)


def sds(*shape):
    return jax.ShapeDtypeStruct(shape, F32)


def iota(shape, dim):
    return lax.broadcasted_iota(jnp.int32, shape, dim)


def front_kernel(
    span, count, state, grad, diag, coup, normal, fnode, stiff, conn, shell_in, sgrad_in, precond_in,
    pack, rim, planes, up, down, shell, sgrad, precond, inverse, faces, elems, sems,
):
    moves = []

    def move(source, target):
        copy = pltpu.make_async_copy(source, target, sems.at[len(moves)])
        copy.start()
        moves.append(copy)

    move(shell_in, shell)
    move(sgrad_in, sgrad)
    move(precond_in, precond)
    move(conn, elems)
    move(fnode, faces)
    move(normal, planes.at[pl.ds(224, 3)])
    move(diag, inverse)
    for j in range(5):
        move(state.at[j], planes.at[pl.ds(16 * j, 16)])
        move(grad.at[j], planes.at[pl.ds(80 + 16 * j, 16)])
    for k in range(3):
        move(coup.at[k], planes.at[pl.ds(176 + 16 * k, 16)])
    early = len(moves)
    for b, (bj, bi) in enumerate(BLOCKS):
        move(stiff.at[pl.ds(8 * bj, 8), pl.ds(8 * bi, 8)], pack.at[pl.ds(8 * b, 8)])
    for copy in moves[:early]:
        copy.wait()
    pack[48] = jnp.zeros((8, 128), F32)
    pack[48, 0:4] = (elems[...] - span[0] * NODE_DEV).astype(F32)
    lead = iota((6, 128), 1) < NB
    zero = jnp.zeros((6, 128), F32)
    rim[0:6, :] = jnp.where(lead, shell[:, 0:128], zero)
    rim[6:12, :] = jnp.where(lead, sgrad[:, 0:128], zero)
    for i in range(6):
        rim[12 + 6 * i : 18 + 6 * i, :] = jnp.where(lead, precond[i, :, 0:128], zero)
    planes[160:176] = 1.0 / inverse[...]
    active = iota((8, 128), 0) * 128 + iota((8, 128), 1) < count[0, 0]
    for i in range(3):
        planes[224 + i] = jnp.where(active, planes[224 + i], 0.0)
    planes[227] = faces[...].astype(F32)
    low = iota((8, 128), 0) < 4

    def body(k, carry):
        a, b = planes[k], planes[k + HALF]
        up[k] = jnp.where(low, pltpu.roll(a, 4, 0), b)
        down[k] = jnp.where(low, a, pltpu.roll(b, 4, 0))
        return carry

    lax.fori_loop(0, HALF, body, 0, unroll=6)
    for copy in moves[early:]:
        copy.wait()


def parts(value):
    high = value.astype(BF16).astype(F32)
    return jnp.concatenate([high, value - high], axis=0).astype(BF16)


def stiff_apply(field, packs, onehot, uvec, fvec):
    for q, pack in enumerate(packs):
        for a in range(4):
            row = pack[48, a : a + 1, :].astype(jnp.int32)
            lane = (4 * q + a) * 128
            hit = iota((EXT, 128), 0) == row
            onehot[:, lane : lane + 128] = jnp.where(hit, 1.0, 0.0).astype(BF16)
    picked = jnp.dot(parts(field), onehot[...], preferred_element_type=F32)
    picked = picked[0:8] + picked[8:16]
    for q, pack in enumerate(packs):
        for a in range(4):
            lane = (4 * q + a) * 128
            uvec[6 * a : 6 * a + 6, :] = picked[0:6, lane : lane + 128]
        out = [jnp.zeros((8, 128), F32) for _ in range(3)]
        for b, (bj, bi) in enumerate(BLOCKS):
            for j in range(8):
                rows = pack[8 * b + j]
                out[bi] = out[bi] + rows * uvec[8 * bj + j : 8 * bj + j + 1, :]
            if bj != bi:
                for i in range(8):
                    rows = pack[8 * b : 8 * b + 8, i, :]
                    out[bj] = out[bj] + rows * uvec[8 * bi + i : 8 * bi + i + 1, :]
        for b in range(3):
            uvec[8 * b : 8 * b + 8, :] = out[b]
        for a in range(4):
            lane = (4 * q + a) * 128
            fvec[0:6, lane : lane + 128] = uvec[6 * a : 6 * a + 6, :]
            fvec[6:8, lane : lane + 128] = jnp.zeros((2, 128), F32)
    forces = lax.dot_general(
        parts(fvec[...]), onehot[...], (((1,), (1,)), ((), ())), preferred_element_type=F32
    )
    return forces[0:8] + forces[8:16]


def first_kernel(
    span, prow, planes, shell, rim, pack,
    own, up, down, down2, faces, nodes, loads, field, onehot, uvec, fvec,
):
    press = prow[0] * planes[0]
    for j in range(1, 5):
        press = press + prow[j] * planes[16 * j]
    local = planes[227].astype(jnp.int32) - (span[0] - 1) * NODE_DEV
    faces[...] = jnp.zeros((8, 1024), F32)
    for r in range(8):
        nodes[0:1, r * 128 : r * 128 + 128] = local[r : r + 1]
    for i in range(3):
        load = planes[224 + i] * press
        for r in range(8):
            faces[i : i + 1, r * 128 : r * 128 + 128] = load[r : r + 1]
    face_parts = parts(faces[...])
    node_row = nodes[0:1, :]

    def chunk(b, carry):
        hit = iota((256, 1024), 0) + b * 256 == node_row
        hot = jnp.where(hit, 1.0, 0.0).astype(BF16)
        got = lax.dot_general(
            face_parts, hot, (((1,), (1,)), ((), ())), preferred_element_type=F32
        )
        got = got[0:8] + got[8:16]
        loads[2 * b] = got[:, 0:128]
        loads[2 * b + 1] = got[:, 128:256]
        return carry

    lax.fori_loop(0, 12, chunk, 0)
    field[...] = jnp.zeros((8, EXT), F32)
    field[0:6, 0:NODE_DEV] = shell[...]
    field[0:6, NODE_DEV:EXT] = rim[0:6, :]
    force = stiff_apply(field[...], (pack,), onehot, uvec, fvec)
    lead = iota((8, 128), 1) < NB
    for t in range(8):
        own[t] = force[:, t * 128 : t * 128 + 128] + loads[8 + t]
        up[t] = loads[16 + t]
        down[t] = loads[t]
    edge = force[:, NODE_DEV:EXT]
    own[8] = edge + jnp.where(lead, loads[16], 0.0)
    up[8] = edge
    down[8] = jnp.where(lead, force[:, 0:128] + loads[8], 0.0)
    down2[...] = jnp.where(lead, loads[0], 0.0)


def precondition(t, precond, rim, res):
    rows = []
    for i in range(6):
        if t < 8:
            block = precond[i, :, t * 128 : t * 128 + 128]
        else:
            block = rim[12 + 6 * i : 18 + 6 * i, :]
        rows.append(jnp.sum(block * res[0:6], axis=0, keepdims=True))
    rows.append(jnp.zeros((2, 128), F32))
    return jnp.concatenate(rows, axis=0)


def shell_residual(first, t, ins):
    if first:
        total, remote, sgrad, rim = ins
        base = sgrad[:, t * 128 : t * 128 + 128] if t < 8 else rim[6:12, :]
        base = jnp.concatenate([base, jnp.zeros((2, 128), F32)], axis=0)
        return base - total[t] - remote[PACKED + t]
    force, rise, fall, prev = ins
    res = prev[t] - force[t]
    if t == 0:
        res = res - rise[...]
    return res - fall[...] if t == 8 else res


def step_kernel(first, *refs):
    refs, (res_out, sum_out, force_out, field, onehot, uvec, fvec) = refs[:-7], refs[-7:]
    own_pack, far_pack, rim, precond, prev_sum = refs[:5]
    for t in range(TILES):
        res = shell_residual(first, t, refs[5:])
        res_out[t] = res
        delta = precondition(t, precond, rim, res)
        sum_out[t] = delta if first else prev_sum[t] + delta
        field[:, t * 128 : t * 128 + 128] = delta
    force = stiff_apply(field[...], (own_pack, far_pack), onehot, uvec, fvec)
    for t in range(TILES):
        force_out[t] = force[:, t * 128 : t * 128 + 128]


def last_kernel(*refs):
    refs, (shell_out, reach_out) = refs[:-2], refs[-2:]
    shell, rim, precond, prev_sum = refs[:4]
    for t in range(8):
        delta = precondition(t, precond, rim, shell_residual(False, t, refs[4:]))
        value = shell[:, t * 128 : t * 128 + 128] + (prev_sum[t] + delta)[0:6]
        shell_out[:, t * 128 : t * 128 + 128] = value
        for i in range(3):
            reach_out[8 * i + t : 8 * i + t + 1, :] = value[i : i + 1]


def pack_chord_kernel(planes, from_lower, from_upper, full, edges):
    low = iota((8, 128), 0) < 4
    full[0:PLANES] = planes[...]

    def unpack(k, carry):
        a, b = from_upper[k], from_lower[k]
        full[PLANES + k] = jnp.where(low, a, pltpu.roll(b, 4, 0))
        full[PLANES + HALF + k] = jnp.where(low, pltpu.roll(a, 4, 0), b)
        return carry

    lax.fori_loop(0, HALF, unpack, 0, unroll=6)
    lane = iota((16, 128), 1)

    def columns(field, count):
        packed = jnp.zeros((16, 128), F32)
        for n in range(count):
            k = 16 * field + n
            value = jnp.concatenate([full[k], full[PLANES + k]], axis=0)
            value = jnp.where(lane < WIDTH, value, pltpu.roll(value, 8, 1))
            value = pltpu.roll(value, 8 * n, 1) if n else value
            packed = jnp.where(lane // 8 == n, value, packed)
        edges[field] = packed

    def one(field, carry):
        columns(field, LAYERS)
        return carry

    lax.fori_loop(0, FIELDS - 1, one, 0)
    columns(FIELDS - 1, 4)


def fluxes(coefs, pairs, upwind, downwind):
    total = [None] * 5
    for k in range(3):
        flux = [None] * 5
        for j in range(5):
            ahead, behind = pairs[k](j)
            for i in range(5):
                term = upwind[k, i, j] * ahead + downwind[k, i, j] * behind
                flux[i] = term if j == 0 else flux[i] + term
        for i in range(5):
            term = coefs[k] * flux[i]
            total[i] = term if k == 0 else total[i] + term
    return total


def sweep(slot, layers, state, halo, first, last, rolled, coef, source, edge_coef, edge_source,
          upwind, downwind, own=None):
    lane = iota((16, 128), 1)

    def layer(n, carry):
        shift = 8 * n
        for j in range(5):
            value, side = state[slot, j, n + 1], halo[slot, j]
            rolled[j, 0] = pltpu.roll(value, 15, 0)
            rolled[j, 1] = pltpu.roll(value, 1, 0)
            rolled[j, 2] = jnp.where(
                lane == 127, pltpu.roll(side, 127 - shift, 1), pltpu.roll(value, 127, 1)
            )
            rolled[j, 3] = jnp.where(
                lane == 0, pltpu.roll(side, 121 - shift, 1), pltpu.roll(value, 1, 1)
            )
            if own is None:
                first[j] = jnp.where(lane == shift + 7, pltpu.roll(value, shift + 7, 1), first[j])
                last[j] = jnp.where(lane == shift, pltpu.roll(value, shift + 1, 1), last[j])
        rows = slice(0, 8) if own is not None else slice(0, 16)
        pairs = (
            lambda j: (state[slot, j, n + 2, rows], state[slot, j, n, rows]),
            lambda j: (rolled[j, 0, rows], rolled[j, 1, rows]),
            lambda j: (rolled[j, 2, rows], rolled[j, 3, rows]),
        )
        total = fluxes([coef(1 + k, n)[rows] for k in range(3)], pairs, upwind, downwind)
        for i in range(5):
            value = coef(0, n)[rows] * (source(i, n)[rows] + total[i])
            if own is not None:
                own(i, n, value)
            else:
                state[1 - slot, i, n + 1] = value
        return carry

    lax.fori_loop(0, layers, layer, 0)
    if own is not None:
        return
    pairs = (
        lambda j: (
            jnp.where(lane < 120, pltpu.roll(halo[slot, j], 120, 1), 0.0),
            jnp.where(lane >= 8, pltpu.roll(halo[slot, j], 8, 1), 0.0),
        ),
        lambda j: (pltpu.roll(halo[slot, j], 15, 0), pltpu.roll(halo[slot, j], 1, 0)),
        lambda j: (
            jnp.where(lane % 8 == 7, first[j], pltpu.roll(halo[slot, j], 127, 1)),
            jnp.where(lane % 8 == 0, last[j], pltpu.roll(halo[slot, j], 1, 1)),
        ),
    )
    total = fluxes([edge_coef(1 + k) for k in range(3)], pairs, upwind, downwind)
    for i in range(5):
        halo[1 - slot, i] = edge_coef(0) * (edge_source(i) + total[i])


def tall(full, k):
    return jnp.concatenate([full[k], full[PLANES + k]], axis=0)


def coef_of(full):
    return lambda k, n: tall(full, 160 + 16 * k + n)


def base_kernel(
    odd, full, near, far, upwind, downwind, out, edge_out, state, halo, first, last, rolled
):
    lane = iota((16, 128), 1)
    right = lane % 8 < WIDTH
    even = odd[0] == 0
    for field in range(FIELDS):
        x, y = near[field], far[field]
        edge_out[field] = jnp.where(right, jnp.where(even, x, y), jnp.where(even, y, x))
    for slot in range(2):
        for j in range(5):
            state[slot, j, 0] = jnp.zeros((16, 128), F32)
            state[slot, j, LAYERS + 1] = jnp.zeros((16, 128), F32)
    for j in range(5):
        halo[0, j] = edge_out[j]
        first[j] = jnp.zeros((16, 128), F32)
        last[j] = jnp.zeros((16, 128), F32)

    def start(n, carry):
        for j in range(5):
            state[0, j, n + 1] = tall(full, 16 * j + n)
        return carry

    lax.fori_loop(0, LAYERS, start, 0)

    def store(i, n, value):
        out[i, n] = value

    for turn in range(SW):
        sweep(
            turn % 2, LAYERS, state, halo, first, last, rolled,
            coef_of(full), lambda i, n: tall(full, 80 + 16 * i + n),
            lambda k: edge_out[10 + k], lambda i: edge_out[5 + i],
            upwind, downwind, store if turn == SW - 1 else None,
        )


def final_kernel(
    span, prow, upwind, downwind, base, full, edges, r0, r1, r2, r3, r4,
    out, reach, state, halo, first, last, rolled,
):
    for b, ref in enumerate((r0, r1, r2, r3, r4)):
        for i in range(3):
            reach[40 * i + 8 * b : 40 * i + 8 * b + 8, :] = ref[8 * i : 8 * i + 8, :]
    walls = edges[FIELDS - 1]
    wall_planes = [pltpu.roll(walls, 128 - 8 * i, 1) if i else walls for i in range(4)]
    node = jnp.concatenate([tall(full, 227), wall_planes[3]], axis=0)
    index = node.astype(jnp.int32) - (span[0] - 2) * NODE_DEV
    block, low = index >> 7, index & 127
    blocks = [block[8 * q : 8 * q + 8] for q in range(4)]
    lows = [low[8 * q : 8 * q + 8] for q in range(4)]

    def pick(h, got):
        got = list(got)
        for i in range(3):
            row = jnp.broadcast_to(reach[pl.ds(40 * i + h, 1), :], (8, 128))
            for q in range(4):
                value = jnp.take_along_axis(row, lows[q], axis=1)
                got[4 * i + q] = jnp.where(blocks[q] == h, value, got[4 * i + q])
        return tuple(got)

    got = lax.fori_loop(
        0, 40, pick, tuple(jnp.zeros((8, 128), F32) for _ in range(12)), unroll=4
    )
    lane = iota((16, 128), 1)
    disp = sum(tall(full, 224 + i) * jnp.concatenate(got[4 * i : 4 * i + 2], axis=0) for i in range(3))
    side = sum(wall_planes[i] * jnp.concatenate(got[4 * i + 2 : 4 * i + 4], axis=0) for i in range(3))
    side = jnp.where(lane < 8, side, 0.0)
    state[...] = jnp.zeros(state.shape, F32)
    for j in range(5):
        state[0, j, 1] = tall(full, 160) * (-prow[j] * disp)
        halo[0, j] = edges[10] * (-prow[j] * side)
        first[j] = jnp.zeros((16, 128), F32)
        last[j] = jnp.zeros((16, 128), F32)
    out[...] = base[...]

    def store(i, n, value):
        out[i, n] = base[i, n] + value

    for turn in range(1, SW):
        sweep(
            (turn + 1) % 2, turn + 1, state, halo, first, last, rolled,
            coef_of(full), lambda i, n: (-prow[i] * jnp.where(n == 0, 1.0, 0.0)) * disp,
            lambda k: edges[10 + k], lambda i: -prow[i] * side,
            upwind, downwind, store if turn == SW - 1 else None,
        )


def along_span(value, steps):
    count = lax.axis_size("span")
    first, last = max(0, -steps), min(count, count - steps)
    return lax.ppermute(value, "span", [(i, i + steps) for i in range(first, last)])


CHORD = ("far_z", "y")


def swap(value, bit):
    count = lax.axis_size(CHORD)
    return lax.ppermute(value, CHORD, [(c, c ^ bit) for c in range(count)])


def ring_sum(value):
    count = lax.axis_size("y")
    pieces = lax.all_to_all(jnp.broadcast_to(value[None], (count, *value.shape)), "y", 0, 0)
    return pieces.sum(0)


def per_device(
    adjoint_flow, flow_grad, diagonal, couplings, upwind, downwind, pressure_row, face_normal,
    face_node, face_count, adjoint_shell, shell_grad, node_precond, element_stiffness, connectivity,
):
    span = lax.axis_index("span").astype(jnp.int32).reshape(1)
    odd = (lax.axis_index("y") % 2).astype(jnp.int32).reshape(1)
    pack, rim, planes, to_upper, to_lower, shell, sgrad, precond = call(
        front_kernel,
        (
            sds(PACKED, 8, 128), sds(48, 128), sds(PLANES, 8, 128), sds(HALF, 8, 128),
            sds(HALF, 8, 128), sds(6, NODE_DEV), sds(6, NODE_DEV), sds(6, 6, NODE_DEV),
        ),
        (
            span, face_count, adjoint_flow, flow_grad, diagonal, couplings, face_normal, face_node,
            element_stiffness, connectivity, adjoint_shell, shell_grad, node_precond,
        ),
        [SM] * 2 + [pl.BlockSpec(memory_space=pltpu.MemorySpace.HBM)] * 11,
        4 << 20,
        (
            pltpu.VMEM((LAYERS, 8, 128), F32), pltpu.VMEM((8, 128), jnp.int32),
            pltpu.VMEM((4, 128), jnp.int32), pltpu.SemaphoreType.DMA((32,)),
        ),
    )
    rim = along_span(rim, -1)
    from_lower, from_upper = along_span(to_upper, 1), along_span(to_lower, -1)
    apply_scratch = lambda nb: (
        pltpu.VMEM((8, EXT), F32),
        pltpu.VMEM((EXT, 512 * nb), BF16),
        pltpu.VMEM((24, 128), F32),
        pltpu.VMEM((8, 512 * nb), F32),
    )
    own, up, down, down2 = call(
        first_kernel,
        (sds(TILES, 8, 128), sds(TILES, 8, 128), sds(TILES, 8, 128), sds(8, 128)),
        (span, pressure_row, planes, shell, rim, pack),
        [SM] * 2 + [VM] * 4,
        8 << 20,
        (pltpu.VMEM((8, 1024), F32), pltpu.VMEM((8, 1024), jnp.int32), pltpu.VMEM((24, 8, 128), F32))
        + apply_scratch(1),
    )
    up, down, down2 = along_span(up, 1), along_span(down, -1), along_span(down2, -2)
    full, edges = call(
        pack_chord_kernel,
        (sds(SLOTS, 8, 128), sds(FIELDS, 16, 128)),
        (planes, from_lower, from_upper),
        [VM] * 3,
        4 << 20,
    )
    near = swap(edges, 1)
    total = own + jnp.concatenate([up[:8] + down[:8], (down[8] + down2)[None]], axis=0)
    total = ring_sum(total.at[0].add(up[8]))
    scratch = lambda layers: (
        pltpu.VMEM((2, 5, layers + 2, 16, 128), F32),
        pltpu.VMEM((2, 5, 16, 128), F32),
        pltpu.VMEM((5, 16, 128), F32),
        pltpu.VMEM((5, 16, 128), F32),
        pltpu.VMEM((5, 4, 16, 128), F32),
    )
    count = lax.axis_size(CHORD)
    pairs = [(c, c - 1 + 2 * (c % 2)) for c in range(1, count - 1)]
    remote = swap(jnp.concatenate([pack, total], axis=0), 4)
    far = lax.ppermute(edges, CHORD, pairs)
    base, edges = call(
        base_kernel,
        (sds(5, LAYERS, 8, 128), sds(FIELDS, 16, 128)),
        (odd, full, near, far, upwind, downwind),
        [SM] + [VM] * 3 + [SM] * 2,
        16 << 20,
        scratch(LAYERS),
    )
    pieces = (total, remote, sgrad, rim)
    res = sums = total
    lead = jnp.arange(128) < NB
    for turn in range(2):
        res, sums, force = call(
            functools.partial(step_kernel, turn == 0),
            (sds(TILES, 8, 128),) * 3,
            (pack, remote if turn == 0 else far_pack, rim, precond, sums) + pieces,
            [VM] * (5 + len(pieces)),
            8 << 20,
            apply_scratch(2),
        )
        far_pack = remote if turn == 0 else far_pack
        force = ring_sum(force)
        rise = along_span(force[8], 1)
        fall = along_span(jnp.where(lead, force[0], 0.0), -1)
        pieces = (force, rise, fall, res)
    shell, reach = call(
        last_kernel,
        (sds(6, NODE_DEV), sds(24, 128)),
        (shell, rim, precond, sums) + pieces,
        [VM] * (4 + len(pieces)),
        1 << 20,
    )
    reaches = [along_span(reach, k) for k in (2, 1)] + [reach] + [along_span(reach, -k) for k in (1, 2)]
    flow = call(
        final_kernel,
        sds(5, LAYERS, 8, 128),
        (span, pressure_row, upwind, downwind, base, full, edges, *reaches),
        [SM] * 4 + [VM] * 8,
        8 << 20,
        (pltpu.VMEM((120, 128), F32), *scratch(SW)),
    )
    return flow, shell


def solution(mesh):
    spans, chords = mesh.devices.shape
    split = Mesh(mesh.devices.reshape(spans, 2, chords // 2), ("span", *CHORD))
    return jax.shard_map(
        per_device,
        mesh=split,
        in_specs=(
            P(None, None, "span", CHORD),
            P(None, None, "span", CHORD),
            P(None, "span", CHORD),
            P(None, None, "span", CHORD),
            P(),
            P(),
            P(),
            P(None, "span", CHORD),
            P("span", CHORD),
            P("span", CHORD),
            P(None, "span"),
            P(None, "span"),
            P(None, None, "span"),
            P(None, None, ("span", *CHORD)),
            P(None, ("span", *CHORD)),
        ),
        out_specs=(P(None, None, "span", CHORD), P(None, "span")),
        check_vma=False,
    )
```

```python
import functools

import jax
import jax.numpy as jnp
from jax import lax
from jax.experimental import pallas as pl
from jax.experimental.pallas import tpu as pltpu
from jax.sharding import Mesh
from jax.sharding import PartitionSpec as P


F32 = jnp.float32
BF16 = jnp.bfloat16
NB = 64
SW = 4
LAYERS = 16
NODE_DEV = 1024
TILES = 9
EXT = TILES * 128
PLANES = 228
HALF = PLANES // 2
FIELDS = 15
SLOTS = 2 * PLANES
WIDTH = 4
PACKED = 49
RING = 4
BLOCKS = ((0, 0), (1, 0), (1, 1), (2, 0), (2, 1), (2, 2))
VM = pl.BlockSpec(memory_space=pltpu.VMEM)
SM = pl.BlockSpec(memory_space=pltpu.SMEM)


def call(body, out, ins, specs, flops, scratch=(), vmem=16):
    return pl.pallas_call(
        body,
        out_shape=out,
        in_specs=specs,
        out_specs=jax.tree.map(lambda _: VM, out),
        scratch_shapes=list(scratch),
        compiler_params=pltpu.CompilerParams(vmem_limit_bytes=vmem << 20),
        cost_estimate=pl.CostEstimate(flops=flops, bytes_accessed=flops // 8, transcendentals=0),
    )(*ins)


def sds(*shape):
    return jax.ShapeDtypeStruct(shape, F32)


def iota(shape, dim):
    return lax.broadcasted_iota(jnp.int32, shape, dim)


def front_kernel(
    span, count, state, grad, diag, coup, normal, fnode, stiff, conn, shell_in, sgrad_in, precond_in,
    pack, rim, planes, up, down, shell, sgrad, precond, walls, inverse, faces, elems, sems,
):
    moves = []

    def move(source, target):
        copy = pltpu.make_async_copy(source, target, sems.at[len(moves)])
        copy.start()
        moves.append(copy)

    move(shell_in, shell)
    move(sgrad_in, sgrad)
    move(precond_in, precond)
    move(conn, elems)
    move(fnode, faces)
    move(normal, planes.at[pl.ds(224, 3)])
    move(diag, inverse)
    for j in range(5):
        move(state.at[j], planes.at[pl.ds(16 * j, 16)])
        move(grad.at[j], planes.at[pl.ds(80 + 16 * j, 16)])
    for k in range(3):
        move(coup.at[k], planes.at[pl.ds(176 + 16 * k, 16)])
    early = len(moves)
    for b, (bj, bi) in enumerate(BLOCKS):
        move(stiff.at[pl.ds(8 * bj, 8), pl.ds(8 * bi, 8)], pack.at[pl.ds(8 * b, 8)])
    for copy in moves[:early]:
        copy.wait()
    pack[48] = jnp.zeros((8, 128), F32)
    pack[48, 0:4] = (elems[...] - span[0] * NODE_DEV).astype(F32)
    lead = iota((6, 128), 1) < NB
    zero = jnp.zeros((6, 128), F32)
    rim[0:6, :] = jnp.where(lead, shell[:, 0:128], zero)
    rim[6:12, :] = jnp.where(lead, sgrad[:, 0:128], zero)
    for i in range(6):
        rim[12 + 6 * i : 18 + 6 * i, :] = jnp.where(lead, precond[i, :, 0:128], zero)
    planes[160:176] = 1.0 / inverse[...]
    active = iota((8, 128), 0) * 128 + iota((8, 128), 1) < count[0, 0]
    for i in range(3):
        planes[224 + i] = jnp.where(active, planes[224 + i], 0.0)
    planes[227] = faces[...].astype(F32)
    for j in range(5):
        walls[j] = planes[16 * j]
    walls[5:9] = planes[224:228]
    low = iota((8, 128), 0) < 4

    def body(k, carry):
        a, b = planes[k], planes[k + HALF]
        up[k] = jnp.where(low, pltpu.roll(a, 4, 0), b)
        down[k] = jnp.where(low, a, pltpu.roll(b, 4, 0))
        return carry

    lax.fori_loop(0, HALF, body, 0, unroll=6)
    for copy in moves[early:]:
        copy.wait()


def parts(value):
    high = value.astype(BF16).astype(F32)
    return jnp.concatenate([high, value - high], axis=0).astype(BF16)


def stiff_apply(field, packs, onehot, uvec, fvec):
    for q, pack in enumerate(packs):
        for a in range(4):
            row = pack[48, a : a + 1, :].astype(jnp.int32)
            lane = (4 * q + a) * 128
            hit = iota((EXT, 128), 0) == row
            onehot[:, lane : lane + 128] = jnp.where(hit, 1.0, 0.0).astype(BF16)
    picked = jnp.dot(parts(field), onehot[...], preferred_element_type=F32)
    picked = picked[0:8] + picked[8:16]
    for q, pack in enumerate(packs):
        for a in range(4):
            lane = (4 * q + a) * 128
            uvec[6 * a : 6 * a + 6, :] = picked[0:6, lane : lane + 128]
        out = [jnp.zeros((8, 128), F32) for _ in range(3)]
        for b, (bj, bi) in enumerate(BLOCKS):
            for j in range(8):
                rows = pack[8 * b + j]
                out[bi] = out[bi] + rows * uvec[8 * bj + j : 8 * bj + j + 1, :]
            if bj != bi:
                for i in range(8):
                    rows = pack[8 * b : 8 * b + 8, i, :]
                    out[bj] = out[bj] + rows * uvec[8 * bi + i : 8 * bi + i + 1, :]
        for b in range(3):
            uvec[8 * b : 8 * b + 8, :] = out[b]
        for a in range(4):
            lane = (4 * q + a) * 128
            fvec[0:6, lane : lane + 128] = uvec[6 * a : 6 * a + 6, :]
            fvec[6:8, lane : lane + 128] = jnp.zeros((2, 128), F32)
    forces = lax.dot_general(
        parts(fvec[...]), onehot[...], (((1,), (1,)), ((), ())), preferred_element_type=F32
    )
    return forces[0:8] + forces[8:16]


def load_kernel(span, prow, walls, loads, faces, nodes):
    press = prow[0] * walls[0]
    for j in range(1, 5):
        press = press + prow[j] * walls[j]
    local = walls[8].astype(jnp.int32) - (span[0] - 1) * NODE_DEV
    faces[...] = jnp.zeros((8, 1024), F32)
    for r in range(8):
        nodes[0:1, r * 128 : r * 128 + 128] = local[r : r + 1]
    for i in range(3):
        load = walls[5 + i] * press
        for r in range(8):
            faces[i : i + 1, r * 128 : r * 128 + 128] = load[r : r + 1]
    face_parts = parts(faces[...])
    node_row = nodes[0:1, :]

    def chunk(b, carry):
        hit = iota((256, 1024), 0) + b * 256 == node_row
        hot = jnp.where(hit, 1.0, 0.0).astype(BF16)
        got = lax.dot_general(
            face_parts, hot, (((1,), (1,)), ((), ())), preferred_element_type=F32
        )
        got = got[0:8] + got[8:16]
        loads[2 * b] = got[:, 0:128]
        loads[2 * b + 1] = got[:, 128:256]
        return carry

    lax.fori_loop(0, 12, chunk, 0)


def first_kernel(loads, shell, rim, pack, own, up, down, down2, field, onehot, uvec, fvec):
    field[...] = jnp.zeros((8, EXT), F32)
    field[0:6, 0:NODE_DEV] = shell[...]
    field[0:6, NODE_DEV:EXT] = rim[0:6, :]
    force = stiff_apply(field[...], (pack,), onehot, uvec, fvec)
    lead = iota((8, 128), 1) < NB
    for t in range(8):
        own[t] = force[:, t * 128 : t * 128 + 128] + loads[8 + t]
        up[t] = loads[16 + t]
        down[t] = loads[t]
    edge = force[:, NODE_DEV:EXT]
    own[8] = edge + jnp.where(lead, loads[16], 0.0)
    up[8] = edge
    down[8] = jnp.where(lead, force[:, 0:128] + loads[8], 0.0)
    down2[...] = jnp.where(lead, loads[0], 0.0)


def precondition(t, precond, rim, res):
    rows = []
    for i in range(6):
        if t < 8:
            block = precond[i, :, t * 128 : t * 128 + 128]
        else:
            block = rim[12 + 6 * i : 18 + 6 * i, :]
        rows.append(jnp.sum(block * res[0:6], axis=0, keepdims=True))
    rows.append(jnp.zeros((2, 128), F32))
    return jnp.concatenate(rows, axis=0)


def shell_residual(first, t, ins):
    if first:
        total, remote, sgrad, rim = ins
        base = sgrad[:, t * 128 : t * 128 + 128] if t < 8 else rim[6:12, :]
        base = jnp.concatenate([base, jnp.zeros((2, 128), F32)], axis=0)
        return base - total[t] - remote[PACKED + t]
    force, prev = ins[:2]
    res = prev[t] - ring_total(force, t)
    if t == 0 and len(ins) > 2:
        res = res - ins[2][...]
    return res - ins[3][...] if t == 8 else res


def ring_total(force, t):
    return (force[0, t] + force[1, t]) + (force[2, t] + force[3, t])


def step_kernel(first, *refs):
    refs, (res_out, sum_out, force_out, field, onehot, uvec, fvec) = refs[:-7], refs[-7:]
    own_pack, far_pack, rim, precond, prev_sum = refs[:5]
    for t in range(TILES):
        res = shell_residual(first, t, refs[5:])
        res_out[t] = res
        delta = precondition(t, precond, rim, res)
        sum_out[t] = delta if first else prev_sum[t] + delta
        field[:, t * 128 : t * 128 + 128] = delta
    force = stiff_apply(field[...], (own_pack, far_pack), onehot, uvec, fvec)
    for t in range(TILES):
        for q in range(RING):
            force_out[q, t] = force[:, t * 128 : t * 128 + 128]


def last_kernel(shell, rim, precond, prev_sum, force, prev, shell_out, reach_out):
    for t in range(8):
        delta = precondition(t, precond, rim, shell_residual(False, t, (force, prev)))
        value = shell[:, t * 128 : t * 128 + 128] + (prev_sum[t] + delta)[0:6]
        shell_out[:, t * 128 : t * 128 + 128] = value
        for i in range(3):
            reach_out[8 * i + t : 8 * i + t + 1, :] = value[i : i + 1]
    reach_out[24:32, :] = -precondition(8, precond, rim, ring_total(force, 8))


def pack_chord_kernel(planes, from_lower, from_upper, full, edges):
    low = iota((8, 128), 0) < 4
    full[0:PLANES] = planes[...]

    def unpack(k, carry):
        a, b = from_upper[k], from_lower[k]
        full[PLANES + k] = jnp.where(low, a, pltpu.roll(b, 4, 0))
        full[PLANES + HALF + k] = jnp.where(low, pltpu.roll(a, 4, 0), b)
        return carry

    lax.fori_loop(0, HALF, unpack, 0, unroll=6)
    lane = iota((16, 128), 1)

    def columns(field, count):
        packed = jnp.zeros((16, 128), F32)
        for n in range(count):
            k = 16 * field + n
            value = jnp.concatenate([full[k], full[PLANES + k]], axis=0)
            value = jnp.where(lane < WIDTH, value, pltpu.roll(value, 8, 1))
            value = pltpu.roll(value, 8 * n, 1) if n else value
            packed = jnp.where(lane // 8 == n, value, packed)
        edges[field] = packed

    def one(field, carry):
        columns(field, LAYERS)
        return carry

    lax.fori_loop(0, FIELDS - 1, one, 0)
    columns(FIELDS - 1, 4)


def fluxes(coefs, pairs, upwind, downwind):
    total = [None] * 5
    for k in range(3):
        flux = [None] * 5
        for j in range(5):
            ahead, behind = pairs[k](j)
            for i in range(5):
                term = upwind[k, i, j] * ahead + downwind[k, i, j] * behind
                flux[i] = term if j == 0 else flux[i] + term
        for i in range(5):
            term = coefs[k] * flux[i]
            total[i] = term if k == 0 else total[i] + term
    return total


def sweep(slot, layers, state, halo, first, last, rolled, coef, source, edge_coef, edge_source,
          upwind, downwind, own=None):
    lane = iota((16, 128), 1)

    def layer(n, carry):
        shift = 8 * n
        for j in range(5):
            value, side = state[slot, j, n + 1], halo[slot, j]
            rolled[j, 0] = pltpu.roll(value, 15, 0)
            rolled[j, 1] = pltpu.roll(value, 1, 0)
            rolled[j, 2] = jnp.where(
                lane == 127, pltpu.roll(side, 127 - shift, 1), pltpu.roll(value, 127, 1)
            )
            rolled[j, 3] = jnp.where(
                lane == 0, pltpu.roll(side, 121 - shift, 1), pltpu.roll(value, 1, 1)
            )
            if own is None:
                first[j] = jnp.where(lane == shift + 7, pltpu.roll(value, shift + 7, 1), first[j])
                last[j] = jnp.where(lane == shift, pltpu.roll(value, shift + 1, 1), last[j])
        rows = slice(0, 8) if own is not None else slice(0, 16)
        pairs = (
            lambda j: (state[slot, j, n + 2, rows], state[slot, j, n, rows]),
            lambda j: (rolled[j, 0, rows], rolled[j, 1, rows]),
            lambda j: (rolled[j, 2, rows], rolled[j, 3, rows]),
        )
        total = fluxes([coef(1 + k, n)[rows] for k in range(3)], pairs, upwind, downwind)
        for i in range(5):
            value = coef(0, n)[rows] * (source(i, n)[rows] + total[i])
            if own is not None:
                own(i, n, value)
            else:
                state[1 - slot, i, n + 1] = value
        return carry

    lax.fori_loop(0, layers, layer, 0)
    if own is not None:
        return
    pairs = (
        lambda j: (
            jnp.where(lane < 120, pltpu.roll(halo[slot, j], 120, 1), 0.0),
            jnp.where(lane >= 8, pltpu.roll(halo[slot, j], 8, 1), 0.0),
        ),
        lambda j: (pltpu.roll(halo[slot, j], 15, 0), pltpu.roll(halo[slot, j], 1, 0)),
        lambda j: (
            jnp.where(lane % 8 == 7, first[j], pltpu.roll(halo[slot, j], 127, 1)),
            jnp.where(lane % 8 == 0, last[j], pltpu.roll(halo[slot, j], 1, 1)),
        ),
    )
    total = fluxes([edge_coef(1 + k) for k in range(3)], pairs, upwind, downwind)
    for i in range(5):
        halo[1 - slot, i] = edge_coef(0) * (edge_source(i) + total[i])


def tall(full, k):
    return jnp.concatenate([full[k], full[PLANES + k]], axis=0)


def coef_of(full):
    return lambda k, n: tall(full, 160 + 16 * k + n)


def base_kernel(
    odd, full, near, far, upwind, downwind, out, edge_out, state, halo, first, last, rolled
):
    lane = iota((16, 128), 1)
    right = lane % 8 < WIDTH
    even = odd[0] == 0
    for field in range(FIELDS):
        x, y = near[field], far[field]
        edge_out[field] = jnp.where(right, jnp.where(even, x, y), jnp.where(even, y, x))
    for slot in range(2):
        for j in range(5):
            state[slot, j, 0] = jnp.zeros((16, 128), F32)
            state[slot, j, LAYERS + 1] = jnp.zeros((16, 128), F32)
    for j in range(5):
        halo[0, j] = edge_out[j]
        first[j] = jnp.zeros((16, 128), F32)
        last[j] = jnp.zeros((16, 128), F32)

    def start(n, carry):
        for j in range(5):
            state[0, j, n + 1] = tall(full, 16 * j + n)
        return carry

    lax.fori_loop(0, LAYERS, start, 0)

    def store(i, n, value):
        out[i, n] = value

    for turn in range(SW):
        sweep(
            turn % 2, LAYERS, state, halo, first, last, rolled,
            coef_of(full), lambda i, n: tall(full, 80 + 16 * i + n),
            lambda k: edge_out[10 + k], lambda i: edge_out[5 + i],
            upwind, downwind, store if turn == SW - 1 else None,
        )


def final_kernel(
    span, prow, upwind, downwind, base, full, edges, r0, r1, r2, r3, r4,
    out, reach, state, halo, first, last, rolled,
):
    for b, ref in enumerate((r0, r1, r2, r3, r4)):
        for i in range(3):
            reach[40 * i + 8 * b : 40 * i + 8 * b + 8, :] = ref[8 * i : 8 * i + 8, :]
    walls = edges[FIELDS - 1]
    wall_planes = [pltpu.roll(walls, 128 - 8 * i, 1) if i else walls for i in range(4)]
    node = jnp.concatenate([tall(full, 227), wall_planes[3]], axis=0)
    index = node.astype(jnp.int32) - (span[0] - 2) * NODE_DEV
    block, low = index >> 7, index & 127
    blocks = [block[8 * q : 8 * q + 8] for q in range(4)]
    lows = [low[8 * q : 8 * q + 8] for q in range(4)]

    def pick(h, got):
        got = list(got)
        for i in range(3):
            row = jnp.broadcast_to(reach[pl.ds(40 * i + h, 1), :], (8, 128))
            for q in range(4):
                value = jnp.take_along_axis(row, lows[q], axis=1)
                got[4 * i + q] = jnp.where(blocks[q] == h, value, got[4 * i + q])
        return tuple(got)

    got = lax.fori_loop(
        0, 40, pick, tuple(jnp.zeros((8, 128), F32) for _ in range(12)), unroll=4
    )
    lane = iota((16, 128), 1)
    disp = sum(tall(full, 224 + i) * jnp.concatenate(got[4 * i : 4 * i + 2], axis=0) for i in range(3))
    side = sum(wall_planes[i] * jnp.concatenate(got[4 * i + 2 : 4 * i + 4], axis=0) for i in range(3))
    side = jnp.where(lane < 8, side, 0.0)
    state[...] = jnp.zeros(state.shape, F32)
    for j in range(5):
        state[0, j, 1] = tall(full, 160) * (-prow[j] * disp)
        halo[0, j] = edges[10] * (-prow[j] * side)
        first[j] = jnp.zeros((16, 128), F32)
        last[j] = jnp.zeros((16, 128), F32)
    out[...] = base[...]

    def store(i, n, value):
        out[i, n] = base[i, n] + value

    for turn in range(1, SW):
        sweep(
            (turn + 1) % 2, turn + 1, state, halo, first, last, rolled,
            coef_of(full), lambda i, n: (-prow[i] * jnp.where(n == 0, 1.0, 0.0)) * disp,
            lambda k: edges[10 + k], lambda i: -prow[i] * side,
            upwind, downwind, store if turn == SW - 1 else None,
        )


def along_span(value, steps):
    count = lax.axis_size("span")
    first, last = max(0, -steps), min(count, count - steps)
    return lax.ppermute(value, "span", [(i, i + steps) for i in range(first, last)])


CHORD = ("far_z", "y")


def swap(value, bit):
    count = lax.axis_size(CHORD)
    return lax.ppermute(value, CHORD, [(c, c ^ bit) for c in range(count)])


def ring_parts(copies):
    return lax.all_to_all(copies, "y", 0, 0)


def per_device(
    adjoint_flow, flow_grad, diagonal, couplings, upwind, downwind, pressure_row, face_normal,
    face_node, face_count, adjoint_shell, shell_grad, node_precond, element_stiffness, connectivity,
):
    span = lax.axis_index("span").astype(jnp.int32).reshape(1)
    odd = (lax.axis_index("y") % 2).astype(jnp.int32).reshape(1)
    pack, rim, planes, to_upper, to_lower, shell, sgrad, precond, walls = call(
        front_kernel,
        (
            sds(PACKED, 8, 128), sds(48, 128), sds(PLANES, 8, 128), sds(HALF, 8, 128),
            sds(HALF, 8, 128), sds(6, NODE_DEV), sds(6, NODE_DEV), sds(6, 6, NODE_DEV),
            sds(9, 8, 128),
        ),
        (
            span, face_count, adjoint_flow, flow_grad, diagonal, couplings, face_normal, face_node,
            element_stiffness, connectivity, adjoint_shell, shell_grad, node_precond,
        ),
        [SM] * 2 + [pl.BlockSpec(memory_space=pltpu.MemorySpace.HBM)] * 11,
        4 << 20,
        (
            pltpu.VMEM((LAYERS, 8, 128), F32), pltpu.VMEM((8, 128), jnp.int32),
            pltpu.VMEM((4, 128), jnp.int32), pltpu.SemaphoreType.DMA((32,)),
        ),
        vmem=60,
    )
    rim = along_span(rim, -1)
    from_lower = along_span(to_upper, 1)
    from_upper = along_span(to_lower, -1)
    loads = call(
        load_kernel,
        sds(24, 8, 128),
        (span, pressure_row, walls),
        [SM] * 2 + [VM],
        4 << 20,
        (pltpu.VMEM((8, 1024), F32), pltpu.VMEM((8, 1024), jnp.int32)),
    )
    apply_scratch = lambda nb: (
        pltpu.VMEM((8, EXT), F32),
        pltpu.VMEM((EXT, 512 * nb), BF16),
        pltpu.VMEM((24, 128), F32),
        pltpu.VMEM((8, 512 * nb), F32),
    )
    own, up, down, down2 = call(
        first_kernel,
        (sds(TILES, 8, 128), sds(TILES, 8, 128), sds(TILES, 8, 128), sds(8, 128)),
        (loads, shell, rim, pack),
        [VM] * 4,
        4 << 20,
        apply_scratch(1),
    )
    up = along_span(up, 1)
    down = along_span(down, -1)
    down2 = along_span(down2, -2)
    full, edges = call(
        pack_chord_kernel,
        (sds(SLOTS, 8, 128), sds(FIELDS, 16, 128)),
        (planes, from_lower, from_upper),
        [VM] * 3,
        4 << 20,
    )
    count = lax.axis_size(CHORD)
    pairs = [(c, c - 1 + 2 * (c % 2)) for c in range(1, count - 1)]
    far = lax.ppermute(edges, CHORD, pairs)
    near = swap(edges, 1)
    total = own + jnp.concatenate([up[:8] + down[:8], (down[8] + down2)[None]], axis=0)
    total = total.at[0].add(up[8])
    total = ring_parts(jnp.broadcast_to(total[None], (RING, *total.shape))).sum(0)
    scratch = lambda layers: (
        pltpu.VMEM((2, 5, layers + 2, 16, 128), F32),
        pltpu.VMEM((2, 5, 16, 128), F32),
        pltpu.VMEM((5, 16, 128), F32),
        pltpu.VMEM((5, 16, 128), F32),
        pltpu.VMEM((5, 4, 16, 128), F32),
    )
    remote = swap(jnp.concatenate([pack, total], axis=0), 4)
    base, edges = call(
        base_kernel,
        (sds(5, LAYERS, 8, 128), sds(FIELDS, 16, 128)),
        (odd, full, near, far, upwind, downwind),
        [SM] + [VM] * 3 + [SM] * 2,
        16 << 20,
        scratch(LAYERS),
    )
    pieces = (total, remote, sgrad, rim)
    res = sums = total
    lead = jnp.arange(128) < NB
    for turn in range(2):
        res, sums, force = call(
            functools.partial(step_kernel, turn == 0),
            (sds(TILES, 8, 128), sds(TILES, 8, 128), sds(RING, TILES, 8, 128)),
            (pack, remote if turn == 0 else far_pack, rim, precond, sums) + pieces,
            [VM] * (5 + len(pieces)),
            8 << 20,
            apply_scratch(2),
        )
        far_pack = remote if turn == 0 else far_pack
        force = ring_parts(force)
        pieces = (force, res)
        if turn == 0:
            pieces += (
                along_span(force[:, 8].sum(0), 1),
                along_span(jnp.where(lead, force[:, 0].sum(0), 0.0), -1),
            )
    shell, reach = call(
        last_kernel,
        (sds(6, NODE_DEV), sds(32, 128)),
        (shell, rim, precond, sums) + pieces,
        [VM] * (4 + len(pieces)),
        1 << 20,
    )
    below, above, lower = along_span(reach, 1), along_span(reach, -1), along_span(reach[24:], 2)
    mend = lambda value, part: (
        value[:24].reshape(3, 8, 128).at[:, 0].add(part[:3]).reshape(24, 128)
    )
    shell = shell.at[:, :128].add(below[24:30])
    reach, below, above = mend(reach, below[24:]), mend(below, lower), mend(above, reach[24:])
    reaches = (along_span(below, 1), below, reach, above, along_span(above, -1))
    flow = call(
        final_kernel,
        sds(5, LAYERS, 8, 128),
        (span, pressure_row, upwind, downwind, base, full, edges, *reaches),
        [SM] * 4 + [VM] * 8,
        8 << 20,
        (pltpu.VMEM((120, 128), F32), *scratch(SW)),
    )
    return flow, shell


def solution(mesh):
    spans, chords = mesh.devices.shape
    split = Mesh(mesh.devices.reshape(spans, 2, chords // 2), ("span", *CHORD))
    return jax.shard_map(
        per_device,
        mesh=split,
        in_specs=(
            P(None, None, "span", CHORD),
            P(None, None, "span", CHORD),
            P(None, "span", CHORD),
            P(None, None, "span", CHORD),
            P(),
            P(),
            P(),
            P(None, "span", CHORD),
            P("span", CHORD),
            P("span", CHORD),
            P(None, "span"),
            P(None, "span"),
            P(None, None, "span"),
            P(None, None, ("span", *CHORD)),
            P(None, ("span", *CHORD)),
        ),
        out_specs=(P(None, None, "span", CHORD), P(None, "span")),
        check_vma=False,
    )
```

```python
import functools

import jax
import jax.numpy as jnp
from jax import lax
from jax.experimental import pallas as pl
from jax.experimental.pallas import tpu as pltpu
from jax.sharding import Mesh
from jax.sharding import PartitionSpec as P


F32 = jnp.float32
BF16 = jnp.bfloat16
NB = 64
SW = 4
LAYERS = 16
NODE_DEV = 1024
TILES = 9
PLANES = 228
HALF = PLANES // 2
FIELDS = 15
SLOTS = 2 * PLANES
WIDTH = 4
PACKED = 49
RING = 4
BLOCKS = ((0, 0), (1, 0), (1, 1), (2, 0), (2, 1), (2, 2))
VM = pl.BlockSpec(memory_space=pltpu.VMEM)
SM = pl.BlockSpec(memory_space=pltpu.SMEM)


def call(body, out, ins, specs, flops, scratch=(), vmem=16):
    return pl.pallas_call(
        body,
        out_shape=out,
        in_specs=specs,
        out_specs=jax.tree.map(lambda _: VM, out),
        scratch_shapes=list(scratch),
        compiler_params=pltpu.CompilerParams(vmem_limit_bytes=vmem << 20),
        cost_estimate=pl.CostEstimate(flops=flops, bytes_accessed=flops // 8, transcendentals=0),
    )(*ins)


def sds(*shape):
    return jax.ShapeDtypeStruct(shape, F32)


def iota(shape, dim):
    return lax.broadcasted_iota(jnp.int32, shape, dim)


def front_kernel(
    span, count, state, grad, diag, coup, normal, fnode, stiff, conn, shell_in, sgrad_in, precond_in,
    pack, rim, planes, up, down, shell, sgrad, precond, walls, inverse, faces, elems, sems,
):
    moves = []

    def move(source, target):
        copy = pltpu.make_async_copy(source, target, sems.at[len(moves)])
        copy.start()
        moves.append(copy)

    move(shell_in, shell)
    move(sgrad_in, sgrad)
    move(precond_in, precond)
    move(conn, elems)
    move(fnode, faces)
    move(normal, planes.at[pl.ds(224, 3)])
    move(diag, inverse)
    for j in range(5):
        move(state.at[j], planes.at[pl.ds(16 * j, 16)])
        move(grad.at[j], planes.at[pl.ds(80 + 16 * j, 16)])
    for k in range(3):
        move(coup.at[k], planes.at[pl.ds(176 + 16 * k, 16)])
    early = len(moves)
    for b, (bj, bi) in enumerate(BLOCKS):
        move(stiff.at[pl.ds(8 * bj, 8), pl.ds(8 * bi, 8)], pack.at[pl.ds(8 * b, 8)])
    for copy in moves[:early]:
        copy.wait()
    pack[48] = jnp.zeros((8, 128), F32)
    pack[48, 0:4] = (elems[...] - span[0] * NODE_DEV).astype(F32)
    lead = iota((6, 128), 1) < NB
    zero = jnp.zeros((6, 128), F32)
    rim[0:6, :] = jnp.where(lead, shell[:, 0:128], zero)
    rim[6:12, :] = jnp.where(lead, sgrad[:, 0:128], zero)
    for i in range(6):
        rim[12 + 6 * i : 18 + 6 * i, :] = jnp.where(lead, precond[i, :, 0:128], zero)
    planes[160:176] = 1.0 / inverse[...]
    active = iota((8, 128), 0) * 128 + iota((8, 128), 1) < count[0, 0]
    for i in range(3):
        planes[224 + i] = jnp.where(active, planes[224 + i], 0.0)
    planes[227] = faces[...].astype(F32)
    for j in range(5):
        walls[j] = planes[16 * j]
    walls[5:9] = planes[224:228]
    low = iota((8, 128), 0) < 4
    even = span[0] % 2 == 0

    def body(k, carry):
        a, b = planes[k], planes[k + HALF]
        to_upper = jnp.where(low, pltpu.roll(a, 4, 0), b)
        to_lower = jnp.where(low, a, pltpu.roll(b, 4, 0))
        up[k] = jnp.where(even, to_upper, to_lower)
        down[k] = jnp.where(even, to_lower, to_upper)
        return carry

    lax.fori_loop(0, HALF, body, 0, unroll=6)
    for copy in moves[early:]:
        copy.wait()


def parts(value):
    high = value.astype(BF16).astype(F32)
    return jnp.concatenate([high, value - high], axis=0).astype(BF16)


def split_index(index, low_hot):
    place = iota(low_hot.shape, 0) == (index & 127)
    low_hot[...] = jnp.where(place, 1.0, 0.0).astype(BF16)
    return index >> 7


def scatter(values, tile, low_hot, tiles):
    spread = jnp.concatenate([jnp.where(tile == t, values, 0.0) for t in range(tiles)], axis=0)
    sums = lax.dot_general(
        parts(spread), low_hot[...], (((1,), (1,)), ((), ())), preferred_element_type=F32
    )
    half = 8 * tiles
    return [sums[8 * t : 8 * t + 8] + sums[half + 8 * t : half + 8 * t + 8] for t in range(tiles)]


def stiff_apply(field, packs, index, low_hot, uvec, fvec):
    for q, pack in enumerate(packs):
        for a in range(4):
            lane = (4 * q + a) * 128
            index[0:1, lane : lane + 128] = pack[48, a : a + 1, :].astype(jnp.int32)
    tile = split_index(index[0:1, :], low_hot)
    found = jnp.dot(
        parts(jnp.concatenate(field, axis=0)), low_hot[...], preferred_element_type=F32
    )
    half = 8 * TILES
    picked = jnp.zeros((8, low_hot.shape[1]), F32)
    for t in range(TILES):
        value = found[8 * t : 8 * t + 8] + found[half + 8 * t : half + 8 * t + 8]
        picked = jnp.where(tile == t, value, picked)
    for q, pack in enumerate(packs):
        for a in range(4):
            lane = (4 * q + a) * 128
            uvec[6 * a : 6 * a + 6, :] = picked[0:6, lane : lane + 128]
        out = [jnp.zeros((8, 128), F32) for _ in range(3)]
        for b, (bj, bi) in enumerate(BLOCKS):
            for j in range(8):
                rows = pack[8 * b + j]
                out[bi] = out[bi] + rows * uvec[8 * bj + j : 8 * bj + j + 1, :]
            if bj != bi:
                for i in range(8):
                    rows = pack[8 * b : 8 * b + 8, i, :]
                    out[bj] = out[bj] + rows * uvec[8 * bi + i : 8 * bi + i + 1, :]
        for b in range(3):
            uvec[8 * b : 8 * b + 8, :] = out[b]
        for a in range(4):
            lane = (4 * q + a) * 128
            fvec[0:6, lane : lane + 128] = uvec[6 * a : 6 * a + 6, :]
            fvec[6:8, lane : lane + 128] = jnp.zeros((2, 128), F32)
    return scatter(fvec[...], tile, low_hot, TILES)


def load_kernel(span, prow, walls, loads, faces, nodes, low_hot):
    press = prow[0] * walls[0]
    for j in range(1, 5):
        press = press + prow[j] * walls[j]
    local = walls[8].astype(jnp.int32) - (span[0] - 1) * NODE_DEV
    faces[...] = jnp.zeros((8, 1024), F32)
    for r in range(8):
        nodes[0:1, r * 128 : r * 128 + 128] = local[r : r + 1]
    for i in range(3):
        load = walls[5 + i] * press
        for r in range(8):
            faces[i : i + 1, r * 128 : r * 128 + 128] = load[r : r + 1]
    tile = split_index(nodes[0:1, :], low_hot)
    for t, value in enumerate(scatter(faces[...], tile, low_hot, 24)):
        loads[t] = value


def first_kernel(
    span, loads, shell, rim, pack, own, inside, across, down2, index, low_hot, uvec, fvec
):
    zero = jnp.zeros((2, 128), F32)
    field = [shell[:, t * 128 : t * 128 + 128] for t in range(8)] + [rim[0:6, :]]
    field = [jnp.concatenate([value, zero], axis=0) for value in field]
    force = stiff_apply(field, (pack,), index, low_hot, uvec, fvec)
    lead = iota((8, 128), 1) < NB
    even = span[0] % 2 == 0

    def send(t, to_upper, to_lower):
        inside[t] = jnp.where(even, to_upper, to_lower)
        across[t] = jnp.where(even, to_lower, to_upper)

    for t in range(8):
        own[t] = force[t] + loads[8 + t]
        send(t, loads[16 + t], loads[t])
    edge = force[8]
    own[8] = edge + jnp.where(lead, loads[16], 0.0)
    send(8, edge, jnp.where(lead, force[0] + loads[8], 0.0))
    down2[...] = jnp.where(lead, loads[0], 0.0)


def precondition(t, precond, rim, res):
    rows = []
    for i in range(6):
        if t < 8:
            block = precond[i, :, t * 128 : t * 128 + 128]
        else:
            block = rim[12 + 6 * i : 18 + 6 * i, :]
        rows.append(jnp.sum(block * res[0:6], axis=0, keepdims=True))
    rows.append(jnp.zeros((2, 128), F32))
    return jnp.concatenate(rows, axis=0)


def shell_residual(first, t, ins):
    if first:
        total, remote, sgrad, rim = ins
        base = sgrad[:, t * 128 : t * 128 + 128] if t < 8 else rim[6:12, :]
        base = jnp.concatenate([base, jnp.zeros((2, 128), F32)], axis=0)
        return base - total[t] - remote[PACKED + t]
    force, prev = ins[:2]
    res = prev[t] - ring_total(force, t)
    if t == 0 and len(ins) > 2:
        res = res - ins[2][...]
    return res - ins[3][...] if t == 8 else res


def ring_total(force, t):
    return (force[0, t] + force[1, t]) + (force[2, t] + force[3, t])


def step_kernel(first, *refs):
    refs, (res_out, sum_out, force_out, index, low_hot, uvec, fvec) = refs[:-7], refs[-7:]
    own_pack, far_pack, rim, precond, prev_sum = refs[:5]
    field = []
    for t in range(TILES):
        res = shell_residual(first, t, refs[5:])
        res_out[t] = res
        delta = precondition(t, precond, rim, res)
        sum_out[t] = delta if first else prev_sum[t] + delta
        field.append(delta)
    force = stiff_apply(field, (own_pack, far_pack), index, low_hot, uvec, fvec)
    for t in range(TILES):
        for q in range(RING):
            force_out[q, t] = force[t]


def last_kernel(shell, rim, precond, prev_sum, force, prev, shell_out, reach_out):
    for t in range(8):
        delta = precondition(t, precond, rim, shell_residual(False, t, (force, prev)))
        value = shell[:, t * 128 : t * 128 + 128] + (prev_sum[t] + delta)[0:6]
        shell_out[:, t * 128 : t * 128 + 128] = value
        for i in range(3):
            reach_out[8 * i + t : 8 * i + t + 1, :] = value[i : i + 1]
    reach_out[24:32, :] = -precondition(8, precond, rim, ring_total(force, 8))


def pack_chord_kernel(span, planes, inside, across, full, edges):
    low = iota((8, 128), 0) < 4
    full[0:PLANES] = planes[...]
    even = span[0] % 2 == 0

    def unpack(k, carry):
        x, y = inside[k], across[k]
        a, b = jnp.where(even, x, y), jnp.where(even, y, x)
        full[PLANES + k] = jnp.where(low, a, pltpu.roll(b, 4, 0))
        full[PLANES + HALF + k] = jnp.where(low, pltpu.roll(a, 4, 0), b)
        return carry

    lax.fori_loop(0, HALF, unpack, 0, unroll=6)
    lane = iota((16, 128), 1)

    def columns(field, count):
        packed = jnp.zeros((16, 128), F32)
        for n in range(count):
            k = 16 * field + n
            value = jnp.concatenate([full[k], full[PLANES + k]], axis=0)
            value = jnp.where(lane < WIDTH, value, pltpu.roll(value, 8, 1))
            value = pltpu.roll(value, 8 * n, 1) if n else value
            packed = jnp.where(lane // 8 == n, value, packed)
        edges[field] = packed

    def one(field, carry):
        columns(field, LAYERS)
        return carry

    lax.fori_loop(0, FIELDS - 1, one, 0)
    columns(FIELDS - 1, 4)


def fluxes(coefs, pairs, upwind, downwind):
    total = [None] * 5
    for k in range(3):
        flux = [None] * 5
        for j in range(5):
            ahead, behind = pairs[k](j)
            for i in range(5):
                term = upwind[k, i, j] * ahead + downwind[k, i, j] * behind
                flux[i] = term if j == 0 else flux[i] + term
        for i in range(5):
            term = coefs[k] * flux[i]
            total[i] = term if k == 0 else total[i] + term
    return total


def sweep(slot, layers, state, halo, first, last, rolled, coef, source, edge_coef, edge_source,
          upwind, downwind, own=None):
    lane = iota((16, 128), 1)

    def layer(n, carry):
        shift = 8 * n
        for j in range(5):
            value, side = state[slot, j, n + 1], halo[slot, j]
            rolled[j, 0] = pltpu.roll(value, 15, 0)
            rolled[j, 1] = pltpu.roll(value, 1, 0)
            rolled[j, 2] = jnp.where(
                lane == 127, pltpu.roll(side, 127 - shift, 1), pltpu.roll(value, 127, 1)
            )
            rolled[j, 3] = jnp.where(
                lane == 0, pltpu.roll(side, 121 - shift, 1), pltpu.roll(value, 1, 1)
            )
            if own is None:
                first[j] = jnp.where(lane == shift + 7, pltpu.roll(value, shift + 7, 1), first[j])
                last[j] = jnp.where(lane == shift, pltpu.roll(value, shift + 1, 1), last[j])
        rows = slice(0, 8) if own is not None else slice(0, 16)
        pairs = (
            lambda j: (state[slot, j, n + 2, rows], state[slot, j, n, rows]),
            lambda j: (rolled[j, 0, rows], rolled[j, 1, rows]),
            lambda j: (rolled[j, 2, rows], rolled[j, 3, rows]),
        )
        total = fluxes([coef(1 + k, n)[rows] for k in range(3)], pairs, upwind, downwind)
        for i in range(5):
            value = coef(0, n)[rows] * (source(i, n)[rows] + total[i])
            if own is not None:
                own(i, n, value)
            else:
                state[1 - slot, i, n + 1] = value
        return carry

    lax.fori_loop(0, layers, layer, 0)
    if own is not None:
        return
    pairs = (
        lambda j: (
            jnp.where(lane < 120, pltpu.roll(halo[slot, j], 120, 1), 0.0),
            jnp.where(lane >= 8, pltpu.roll(halo[slot, j], 8, 1), 0.0),
        ),
        lambda j: (pltpu.roll(halo[slot, j], 15, 0), pltpu.roll(halo[slot, j], 1, 0)),
        lambda j: (
            jnp.where(lane % 8 == 7, first[j], pltpu.roll(halo[slot, j], 127, 1)),
            jnp.where(lane % 8 == 0, last[j], pltpu.roll(halo[slot, j], 1, 1)),
        ),
    )
    total = fluxes([edge_coef(1 + k) for k in range(3)], pairs, upwind, downwind)
    for i in range(5):
        halo[1 - slot, i] = edge_coef(0) * (edge_source(i) + total[i])


def tall(full, k):
    return jnp.concatenate([full[k], full[PLANES + k]], axis=0)


def coef_of(full):
    return lambda k, n: tall(full, 160 + 16 * k + n)


def base_kernel(
    odd, full, near, far, upwind, downwind, out, edge_out, state, halo, first, last, rolled
):
    lane = iota((16, 128), 1)
    right = lane % 8 < WIDTH
    even = odd[0] == 0
    for field in range(FIELDS):
        x, y = near[field], far[field]
        edge_out[field] = jnp.where(right, jnp.where(even, x, y), jnp.where(even, y, x))
    for slot in range(2):
        for j in range(5):
            state[slot, j, 0] = jnp.zeros((16, 128), F32)
            state[slot, j, LAYERS + 1] = jnp.zeros((16, 128), F32)
    for j in range(5):
        halo[0, j] = edge_out[j]
        first[j] = jnp.zeros((16, 128), F32)
        last[j] = jnp.zeros((16, 128), F32)

    def start(n, carry):
        for j in range(5):
            state[0, j, n + 1] = tall(full, 16 * j + n)
        return carry

    lax.fori_loop(0, LAYERS, start, 0)

    def store(i, n, value):
        out[i, n] = value

    for turn in range(SW):
        sweep(
            turn % 2, LAYERS, state, halo, first, last, rolled,
            coef_of(full), lambda i, n: tall(full, 80 + 16 * i + n),
            lambda k: edge_out[10 + k], lambda i: edge_out[5 + i],
            upwind, downwind, store if turn == SW - 1 else None,
        )


def final_kernel(
    span, prow, upwind, downwind, base, full, edges, across, r1, r2, r3, inside, shell, part,
    out, shell_out, reach, state, halo, first, last, rolled,
):
    shell_out[...] = shell[...]
    shell_out[:, 0:128] = shell[:, 0:128] + part[24:30, :]
    even = span[0] % 2 == 0
    x, y = across[...], inside[...]
    blocks = (jnp.where(even, x, y), r1[...], r2[...], r3[...], jnp.where(even, y, x))
    for b, value in enumerate(blocks):
        for i in range(3):
            reach[40 * i + 8 * b : 40 * i + 8 * b + 8, :] = value[8 * i : 8 * i + 8]
    walls = edges[FIELDS - 1]
    wall_planes = [pltpu.roll(walls, 128 - 8 * i, 1) if i else walls for i in range(4)]
    node = jnp.concatenate([tall(full, 227), wall_planes[3]], axis=0)
    index = node.astype(jnp.int32) - (span[0] - 2) * NODE_DEV
    block, low = index >> 7, index & 127
    blocks = [block[8 * q : 8 * q + 8] for q in range(4)]
    lows = [low[8 * q : 8 * q + 8] for q in range(4)]

    def pick(h, got):
        got = list(got)
        for i in range(3):
            row = jnp.broadcast_to(reach[pl.ds(40 * i + h, 1), :], (8, 128))
            for q in range(4):
                value = jnp.take_along_axis(row, lows[q], axis=1)
                got[4 * i + q] = jnp.where(blocks[q] == h, value, got[4 * i + q])
        return tuple(got)

    got = lax.fori_loop(
        0, 40, pick, tuple(jnp.zeros((8, 128), F32) for _ in range(12)), unroll=4
    )
    lane = iota((16, 128), 1)
    disp = sum(tall(full, 224 + i) * jnp.concatenate(got[4 * i : 4 * i + 2], axis=0) for i in range(3))
    side = sum(wall_planes[i] * jnp.concatenate(got[4 * i + 2 : 4 * i + 4], axis=0) for i in range(3))
    side = jnp.where(lane < 8, side, 0.0)
    state[...] = jnp.zeros(state.shape, F32)
    for j in range(5):
        state[0, j, 1] = tall(full, 160) * (-prow[j] * disp)
        halo[0, j] = edges[10] * (-prow[j] * side)
        first[j] = jnp.zeros((16, 128), F32)
        last[j] = jnp.zeros((16, 128), F32)
    out[...] = base[...]

    def store(i, n, value):
        out[i, n] = base[i, n] + value

    for turn in range(1, SW):
        sweep(
            (turn + 1) % 2, turn + 1, state, halo, first, last, rolled,
            coef_of(full), lambda i, n: (-prow[i] * jnp.where(n == 0, 1.0, 0.0)) * disp,
            lambda k: edges[10 + k], lambda i: -prow[i] * side,
            upwind, downwind, store if turn == SW - 1 else None,
        )


def along_span(value, steps):
    count = lax.axis_size("span")
    first, last = max(0, -steps), min(count, count - steps)
    return lax.ppermute(value, "span", [(i, i + steps) for i in range(first, last)])


def exchange(to_upper, to_lower):
    even = lax.axis_index("span") % 2 == 0
    count = lax.axis_size("span")
    across = jnp.where(even, to_lower, to_upper)
    across = lax.ppermute(across, "span", cross_pairs(count))
    inside = jnp.where(even, to_upper, to_lower)
    inside = lax.ppermute(inside, "span", inside_pairs(count))
    return jnp.where(even, across, inside), jnp.where(even, inside, across)


def cross_pairs(count):
    return [(s, s - 1 + 2 * (s % 2)) for s in range(1, count - 1)]


def inside_pairs(count):
    return [(s, s ^ 1) for s in range(count)]


CHORD = ("far_z", "y")


def swap(value, bit):
    count = lax.axis_size(CHORD)
    return lax.ppermute(value, CHORD, [(c, c ^ bit) for c in range(count)])


def ring_parts(copies):
    return lax.all_to_all(copies, "y", 0, 0)


def per_device(
    adjoint_flow, flow_grad, diagonal, couplings, upwind, downwind, pressure_row, face_normal,
    face_node, face_count, adjoint_shell, shell_grad, node_precond, element_stiffness, connectivity,
):
    span = lax.axis_index("span").astype(jnp.int32).reshape(1)
    odd = (lax.axis_index("y") % 2).astype(jnp.int32).reshape(1)
    pack, rim, planes, to_inside, to_across, shell, sgrad, precond, walls = call(
        front_kernel,
        (
            sds(PACKED, 8, 128), sds(48, 128), sds(PLANES, 8, 128), sds(HALF, 8, 128),
            sds(HALF, 8, 128), sds(6, NODE_DEV), sds(6, NODE_DEV), sds(6, 6, NODE_DEV),
            sds(9, 8, 128),
        ),
        (
            span, face_count, adjoint_flow, flow_grad, diagonal, couplings, face_normal, face_node,
            element_stiffness, connectivity, adjoint_shell, shell_grad, node_precond,
        ),
        [SM] * 2 + [pl.BlockSpec(memory_space=pltpu.MemorySpace.HBM)] * 11,
        4 << 20,
        (
            pltpu.VMEM((LAYERS, 8, 128), F32), pltpu.VMEM((8, 128), jnp.int32),
            pltpu.VMEM((4, 128), jnp.int32), pltpu.SemaphoreType.DMA((32,)),
        ),
        vmem=60,
    )
    rim = along_span(rim, -1)
    spans = lax.axis_size("span")
    halo_across = lax.ppermute(to_across, "span", cross_pairs(spans))
    halo_inside = lax.ppermute(to_inside, "span", inside_pairs(spans))
    loads = call(
        load_kernel,
        sds(24, 8, 128),
        (span, pressure_row, walls),
        [SM] * 2 + [VM],
        4 << 20,
        (
            pltpu.VMEM((8, 1024), F32),
            pltpu.VMEM((8, 1024), jnp.int32),
            pltpu.VMEM((128, 1024), BF16),
        ),
    )
    apply_scratch = lambda nb: (
        pltpu.VMEM((8, 512 * nb), jnp.int32),
        pltpu.VMEM((128, 512 * nb), BF16),
        pltpu.VMEM((24, 128), F32),
        pltpu.VMEM((8, 512 * nb), F32),
    )
    own, inside, across, down2 = call(
        first_kernel,
        (sds(TILES, 8, 128), sds(TILES, 8, 128), sds(TILES, 8, 128), sds(8, 128)),
        (span, loads, shell, rim, pack),
        [SM] + [VM] * 4,
        4 << 20,
        apply_scratch(1),
    )
    across = lax.ppermute(across, "span", cross_pairs(spans))
    inside = lax.ppermute(inside, "span", inside_pairs(spans))
    even = span[0] % 2 == 0
    up, down = jnp.where(even, across, inside), jnp.where(even, inside, across)
    down2 = along_span(down2, -2)
    full, edges = call(
        pack_chord_kernel,
        (sds(SLOTS, 8, 128), sds(FIELDS, 16, 128)),
        (span, planes, halo_inside, halo_across),
        [SM] + [VM] * 3,
        4 << 20,
    )
    count = lax.axis_size(CHORD)
    pairs = [(c, c - 1 + 2 * (c % 2)) for c in range(1, count - 1)]
    far = lax.ppermute(edges, CHORD, pairs)
    near = swap(edges, 1)
    total = own + jnp.concatenate([up[:8] + down[:8], (down[8] + down2)[None]], axis=0)
    total = total.at[0].add(up[8])
    total = ring_parts(jnp.broadcast_to(total[None], (RING, *total.shape))).sum(0)
    scratch = lambda layers: (
        pltpu.VMEM((2, 5, layers + 2, 16, 128), F32),
        pltpu.VMEM((2, 5, 16, 128), F32),
        pltpu.VMEM((5, 16, 128), F32),
        pltpu.VMEM((5, 16, 128), F32),
        pltpu.VMEM((5, 4, 16, 128), F32),
    )
    remote = swap(jnp.concatenate([pack, total], axis=0), 4)
    base, edges = call(
        base_kernel,
        (sds(5, LAYERS, 8, 128), sds(FIELDS, 16, 128)),
        (odd, full, near, far, upwind, downwind),
        [SM] + [VM] * 3 + [SM] * 2,
        16 << 20,
        scratch(LAYERS),
    )
    pieces = (total, remote, sgrad, rim)
    res = sums = total
    lead = jnp.arange(128) < NB
    for turn in range(2):
        res, sums, force = call(
            functools.partial(step_kernel, turn == 0),
            (sds(TILES, 8, 128), sds(TILES, 8, 128), sds(RING, TILES, 8, 128)),
            (pack, remote if turn == 0 else far_pack, rim, precond, sums) + pieces,
            [VM] * (5 + len(pieces)),
            8 << 20,
            apply_scratch(2),
        )
        far_pack = remote if turn == 0 else far_pack
        force = ring_parts(force)
        pieces = (force, res)
        if turn == 0:
            pieces += exchange(force[:, 8].sum(0), jnp.where(lead, force[:, 0].sum(0), 0.0))
    shell, reach = call(
        last_kernel,
        (sds(6, NODE_DEV), sds(32, 128)),
        (shell, rim, precond, sums) + pieces,
        [VM] * (4 + len(pieces)),
        1 << 20,
    )
    lower = along_span(reach[24:], 2)
    below, above = exchange(reach, reach)
    mend = lambda value, part: (
        value[:24].reshape(3, 8, 128).at[:, 0].add(part[:3]).reshape(24, 128)
    )
    part = below
    reach, below, above = mend(reach, below[24:]), mend(below, lower), mend(above, reach[24:])
    even = span[0] % 2 == 0
    across = lax.ppermute(jnp.where(even, above, below), "span", cross_pairs(spans))
    inside = lax.ppermute(jnp.where(even, below, above), "span", inside_pairs(spans))
    reaches = (across, below, reach, above, inside, shell, part)
    flow, shell = call(
        final_kernel,
        (sds(5, LAYERS, 8, 128), sds(6, NODE_DEV)),
        (span, pressure_row, upwind, downwind, base, full, edges, *reaches),
        [SM] * 4 + [VM] * 10,
        8 << 20,
        (pltpu.VMEM((120, 128), F32), *scratch(SW)),
    )
    return flow, shell


def solution(mesh):
    spans, chords = mesh.devices.shape
    split = Mesh(mesh.devices.reshape(spans, 2, chords // 2), ("span", *CHORD))
    return jax.shard_map(
        per_device,
        mesh=split,
        in_specs=(
            P(None, None, "span", CHORD),
            P(None, None, "span", CHORD),
            P(None, "span", CHORD),
            P(None, None, "span", CHORD),
            P(),
            P(),
            P(),
            P(None, "span", CHORD),
            P("span", CHORD),
            P("span", CHORD),
            P(None, "span"),
            P(None, "span"),
            P(None, None, "span"),
            P(None, None, ("span", *CHORD)),
            P(None, ("span", *CHORD)),
        ),
        out_specs=(P(None, None, "span", CHORD), P(None, "span")),
        check_vma=False,
    )
```

```python
import functools

import jax
import jax.numpy as jnp
from jax import lax
from jax.experimental import pallas as pl
from jax.experimental.pallas import tpu as pltpu
from jax.sharding import Mesh
from jax.sharding import PartitionSpec as P


F32 = jnp.float32
BF16 = jnp.bfloat16
NB = 64
SW = 4
LAYERS = 16
NODE_DEV = 1024
TILES = 9
PLANES = 228
HALF = PLANES // 2
FIELDS = 15
SLOTS = 2 * PLANES
WIDTH = 4
PACKED = 49
RING = 4
BLOCKS = ((0, 0), (1, 0), (1, 1), (2, 0), (2, 1), (2, 2))
VM = pl.BlockSpec(memory_space=pltpu.VMEM)
SM = pl.BlockSpec(memory_space=pltpu.SMEM)


def call(body, out, ins, specs, flops, scratch=(), vmem=16):
    return pl.pallas_call(
        body,
        out_shape=out,
        in_specs=specs,
        out_specs=jax.tree.map(lambda _: VM, out),
        scratch_shapes=list(scratch),
        compiler_params=pltpu.CompilerParams(vmem_limit_bytes=vmem << 20),
        cost_estimate=pl.CostEstimate(flops=flops, bytes_accessed=flops // 8, transcendentals=0),
    )(*ins)


def sds(*shape):
    return jax.ShapeDtypeStruct(shape, F32)


def iota(shape, dim):
    return lax.broadcasted_iota(jnp.int32, shape, dim)


def front_kernel(
    span, count, state, grad, diag, coup, normal, fnode, stiff, conn, shell_in, sgrad_in, precond_in,
    pack, rim, planes, up, down, shell, sgrad, precond, walls, inverse, faces, elems, sems,
):
    moves = []

    def move(source, target):
        copy = pltpu.make_async_copy(source, target, sems.at[len(moves)])
        copy.start()
        moves.append(copy)

    move(shell_in, shell)
    move(sgrad_in, sgrad)
    move(precond_in, precond)
    move(conn, elems)
    move(fnode, faces)
    move(normal, planes.at[pl.ds(224, 3)])
    move(diag, inverse)
    for j in range(5):
        move(state.at[j], planes.at[pl.ds(16 * j, 16)])
        move(grad.at[j], planes.at[pl.ds(80 + 16 * j, 16)])
    for k in range(3):
        move(coup.at[k], planes.at[pl.ds(176 + 16 * k, 16)])
    early = len(moves)
    for b, (bj, bi) in enumerate(BLOCKS):
        move(stiff.at[pl.ds(8 * bj, 8), pl.ds(8 * bi, 8)], pack.at[pl.ds(8 * b, 8)])
    for copy in moves[:early]:
        copy.wait()
    pack[48] = jnp.zeros((8, 128), F32)
    pack[48, 0:4] = (elems[...] - span[0] * NODE_DEV).astype(F32)
    lead = iota((6, 128), 1) < NB
    zero = jnp.zeros((6, 128), F32)
    rim[0:6, :] = jnp.where(lead, shell[:, 0:128], zero)
    rim[6:12, :] = jnp.where(lead, sgrad[:, 0:128], zero)
    for i in range(6):
        rim[12 + 6 * i : 18 + 6 * i, :] = jnp.where(lead, precond[i, :, 0:128], zero)
    planes[160:176] = 1.0 / inverse[...]
    active = iota((8, 128), 0) * 128 + iota((8, 128), 1) < count[0, 0]
    for i in range(3):
        planes[224 + i] = jnp.where(active, planes[224 + i], 0.0)
    planes[227] = faces[...].astype(F32)
    for j in range(5):
        walls[j] = planes[16 * j]
    walls[5:9] = planes[224:228]
    low = iota((8, 128), 0) < 4
    even = span[0] % 2 == 0

    def body(k, carry):
        a, b = planes[k], planes[k + HALF]
        to_upper = jnp.where(low, pltpu.roll(a, 4, 0), b)
        to_lower = jnp.where(low, a, pltpu.roll(b, 4, 0))
        up[k] = jnp.where(even, to_upper, to_lower)
        down[k] = jnp.where(even, to_lower, to_upper)
        return carry

    lax.fori_loop(0, HALF, body, 0, unroll=6)
    for copy in moves[early:]:
        copy.wait()


def parts(value):
    high = value.astype(BF16).astype(F32)
    return jnp.concatenate([high, value - high], axis=0).astype(BF16)


def split_index(index, low_hot):
    place = iota(low_hot.shape, 0) == (index & 127)
    low_hot[...] = jnp.where(place, 1.0, 0.0).astype(BF16)
    return index >> 7


def scatter(values, tile, low_hot, tiles):
    spread = jnp.concatenate([jnp.where(tile == t, values, 0.0) for t in range(tiles)], axis=0)
    sums = lax.dot_general(
        parts(spread), low_hot[...], (((1,), (1,)), ((), ())), preferred_element_type=F32
    )
    half = 8 * tiles
    return [sums[8 * t : 8 * t + 8] + sums[half + 8 * t : half + 8 * t + 8] for t in range(tiles)]


def stiff_apply(field, packs, index, low_hot, uvec, fvec):
    for q, pack in enumerate(packs):
        for a in range(4):
            lane = (4 * q + a) * 128
            index[0:1, lane : lane + 128] = pack[48, a : a + 1, :].astype(jnp.int32)
    tile = split_index(index[0:1, :], low_hot)
    found = jnp.dot(
        parts(jnp.concatenate(field, axis=0)), low_hot[...], preferred_element_type=F32
    )
    half = 8 * TILES
    picked = jnp.zeros((8, low_hot.shape[1]), F32)
    for t in range(TILES):
        value = found[8 * t : 8 * t + 8] + found[half + 8 * t : half + 8 * t + 8]
        picked = jnp.where(tile == t, value, picked)
    for q, pack in enumerate(packs):
        for a in range(4):
            lane = (4 * q + a) * 128
            uvec[6 * a : 6 * a + 6, :] = picked[0:6, lane : lane + 128]
        out = [jnp.zeros((8, 128), F32) for _ in range(3)]
        for b, (bj, bi) in enumerate(BLOCKS):
            for j in range(8):
                rows = pack[8 * b + j]
                out[bi] = out[bi] + rows * uvec[8 * bj + j : 8 * bj + j + 1, :]
            if bj != bi:
                for i in range(8):
                    rows = pack[8 * b : 8 * b + 8, i, :]
                    out[bj] = out[bj] + rows * uvec[8 * bi + i : 8 * bi + i + 1, :]
        for b in range(3):
            uvec[8 * b : 8 * b + 8, :] = out[b]
        for a in range(4):
            lane = (4 * q + a) * 128
            fvec[0:6, lane : lane + 128] = uvec[6 * a : 6 * a + 6, :]
            fvec[6:8, lane : lane + 128] = jnp.zeros((2, 128), F32)
    return scatter(fvec[...], tile, low_hot, TILES)


def load_kernel(span, prow, walls, loads, faces, nodes, low_hot):
    press = prow[0] * walls[0]
    for j in range(1, 5):
        press = press + prow[j] * walls[j]
    local = walls[8].astype(jnp.int32) - (span[0] - 1) * NODE_DEV
    faces[...] = jnp.zeros((8, 1024), F32)
    for r in range(8):
        nodes[0:1, r * 128 : r * 128 + 128] = local[r : r + 1]
    for i in range(3):
        load = walls[5 + i] * press
        for r in range(8):
            faces[i : i + 1, r * 128 : r * 128 + 128] = load[r : r + 1]
    tile = split_index(nodes[0:1, :], low_hot)
    for t, value in enumerate(scatter(faces[...], tile, low_hot, 24)):
        loads[t] = value


def first_kernel(
    span, loads, shell, rim, pack, own, inside, across, down2, index, low_hot, uvec, fvec
):
    zero = jnp.zeros((2, 128), F32)
    field = [shell[:, t * 128 : t * 128 + 128] for t in range(8)] + [rim[0:6, :]]
    field = [jnp.concatenate([value, zero], axis=0) for value in field]
    force = stiff_apply(field, (pack,), index, low_hot, uvec, fvec)
    lead = iota((8, 128), 1) < NB
    even = span[0] % 2 == 0

    def send(t, to_upper, to_lower):
        inside[t] = jnp.where(even, to_upper, to_lower)
        across[t] = jnp.where(even, to_lower, to_upper)

    for t in range(8):
        own[t] = force[t] + loads[8 + t]
        send(t, loads[16 + t], loads[t])
    edge = force[8]
    own[8] = edge + jnp.where(lead, loads[16], 0.0)
    send(8, edge, jnp.where(lead, force[0] + loads[8], 0.0))
    down2[...] = jnp.where(lead, loads[0], 0.0)


def precondition(t, precond, rim, res):
    rows = []
    for i in range(6):
        if t < 8:
            block = precond[i, :, t * 128 : t * 128 + 128]
        else:
            block = rim[12 + 6 * i : 18 + 6 * i, :]
        rows.append(jnp.sum(block * res[0:6], axis=0, keepdims=True))
    rows.append(jnp.zeros((2, 128), F32))
    return jnp.concatenate(rows, axis=0)


def shell_residual(first, t, ins):
    if first:
        total, remote, sgrad, rim = ins
        base = sgrad[:, t * 128 : t * 128 + 128] if t < 8 else rim[6:12, :]
        base = jnp.concatenate([base, jnp.zeros((2, 128), F32)], axis=0)
        return base - total[t] - remote[PACKED + t]
    force, prev = ins[:2]
    res = prev[t] - ring_total(force, t)
    if t == 0 and len(ins) > 2:
        res = res - ins[2][...]
    return res - ins[3][...] if t == 8 else res


def ring_total(force, t):
    return (force[0, t] + force[1, t]) + (force[2, t] + force[3, t])


def step_kernel(first, *refs):
    refs, (res_out, sum_out, force_out, index, low_hot, uvec, fvec) = refs[:-7], refs[-7:]
    own_pack, far_pack, rim, precond, prev_sum = refs[:5]
    field = []
    for t in range(TILES):
        res = shell_residual(first, t, refs[5:])
        res_out[t] = res
        delta = precondition(t, precond, rim, res)
        sum_out[t] = delta if first else prev_sum[t] + delta
        field.append(delta)
    force = stiff_apply(field, (own_pack, far_pack), index, low_hot, uvec, fvec)
    for t in range(TILES):
        for q in range(RING):
            force_out[q, t] = force[t]


def last_kernel(shell, rim, precond, prev_sum, force, prev, shell_out, reach_out):
    for t in range(8):
        delta = precondition(t, precond, rim, shell_residual(False, t, (force, prev)))
        value = shell[:, t * 128 : t * 128 + 128] + (prev_sum[t] + delta)[0:6]
        shell_out[:, t * 128 : t * 128 + 128] = value
        for i in range(3):
            reach_out[8 * i + t : 8 * i + t + 1, :] = value[i : i + 1]
    reach_out[24:32, :] = -precondition(8, precond, rim, ring_total(force, 8))


def pack_chord_kernel(span, planes, inside, across, full, edges):
    low = iota((8, 128), 0) < 4
    full[0:PLANES] = planes[...]
    even = span[0] % 2 == 0

    def unpack(k, carry):
        x, y = inside[k], across[k]
        a, b = jnp.where(even, x, y), jnp.where(even, y, x)
        full[PLANES + k] = jnp.where(low, a, pltpu.roll(b, 4, 0))
        full[PLANES + HALF + k] = jnp.where(low, pltpu.roll(a, 4, 0), b)
        return carry

    lax.fori_loop(0, HALF, unpack, 0, unroll=6)
    lane = iota((16, 128), 1)

    def columns(field, count):
        packed = jnp.zeros((16, 128), F32)
        for n in range(count):
            k = 16 * field + n
            value = jnp.concatenate([full[k], full[PLANES + k]], axis=0)
            value = jnp.where(lane < WIDTH, value, pltpu.roll(value, 8, 1))
            value = pltpu.roll(value, 8 * n, 1) if n else value
            packed = jnp.where(lane // 8 == n, value, packed)
        edges[field] = packed

    def one(field, carry):
        columns(field, LAYERS)
        return carry

    lax.fori_loop(0, FIELDS - 1, one, 0)
    columns(FIELDS - 1, 4)


def fluxes(coefs, pairs, upwind, downwind):
    total = [None] * 5
    for k in range(3):
        flux = [None] * 5
        for j in range(5):
            ahead, behind = pairs[k](j)
            for i in range(5):
                term = upwind[k, i, j] * ahead + downwind[k, i, j] * behind
                flux[i] = term if j == 0 else flux[i] + term
        for i in range(5):
            term = coefs[k] * flux[i]
            total[i] = term if k == 0 else total[i] + term
    return total


def sweep(slot, layers, state, halo, first, last, rolled, coef, source, edge_coef, edge_source,
          upwind, downwind, own=None):
    lane = iota((16, 128), 1)

    def layer(n, carry):
        shift = 8 * n
        for j in range(5):
            value, side = state[slot, j, n + 1], halo[slot, j]
            rolled[j, 0] = pltpu.roll(value, 15, 0)
            rolled[j, 1] = pltpu.roll(value, 1, 0)
            rolled[j, 2] = jnp.where(
                lane == 127, pltpu.roll(side, 127 - shift, 1), pltpu.roll(value, 127, 1)
            )
            rolled[j, 3] = jnp.where(
                lane == 0, pltpu.roll(side, 121 - shift, 1), pltpu.roll(value, 1, 1)
            )
            if own is None:
                first[j] = jnp.where(lane == shift + 7, pltpu.roll(value, shift + 7, 1), first[j])
                last[j] = jnp.where(lane == shift, pltpu.roll(value, shift + 1, 1), last[j])
        rows = slice(0, 8) if own is not None else slice(0, 16)
        pairs = (
            lambda j: (state[slot, j, n + 2, rows], state[slot, j, n, rows]),
            lambda j: (rolled[j, 0, rows], rolled[j, 1, rows]),
            lambda j: (rolled[j, 2, rows], rolled[j, 3, rows]),
        )
        total = fluxes([coef(1 + k, n)[rows] for k in range(3)], pairs, upwind, downwind)
        for i in range(5):
            value = coef(0, n)[rows] * (source(i, n)[rows] + total[i])
            if own is not None:
                own(i, n, value)
            else:
                state[1 - slot, i, n + 1] = value
        return carry

    lax.fori_loop(0, layers, layer, 0)
    if own is not None:
        return
    pairs = (
        lambda j: (
            jnp.where(lane < 120, pltpu.roll(halo[slot, j], 120, 1), 0.0),
            jnp.where(lane >= 8, pltpu.roll(halo[slot, j], 8, 1), 0.0),
        ),
        lambda j: (pltpu.roll(halo[slot, j], 15, 0), pltpu.roll(halo[slot, j], 1, 0)),
        lambda j: (
            jnp.where(lane % 8 == 7, first[j], pltpu.roll(halo[slot, j], 127, 1)),
            jnp.where(lane % 8 == 0, last[j], pltpu.roll(halo[slot, j], 1, 1)),
        ),
    )
    total = fluxes([edge_coef(1 + k) for k in range(3)], pairs, upwind, downwind)
    for i in range(5):
        halo[1 - slot, i] = edge_coef(0) * (edge_source(i) + total[i])


def tall(full, k):
    return jnp.concatenate([full[k], full[PLANES + k]], axis=0)


def coef_of(full):
    return lambda k, n: tall(full, 160 + 16 * k + n)


def base_kernel(
    odd, full, near, far, upwind, downwind, out, edge_out, state, halo, first, last, rolled
):
    lane = iota((16, 128), 1)
    right = lane % 8 < WIDTH
    even = odd[0] == 0
    for field in range(FIELDS):
        x, y = near[field], far[field]
        edge_out[field] = jnp.where(right, jnp.where(even, x, y), jnp.where(even, y, x))
    for slot in range(2):
        for j in range(5):
            state[slot, j, 0] = jnp.zeros((16, 128), F32)
            state[slot, j, LAYERS + 1] = jnp.zeros((16, 128), F32)
    for j in range(5):
        halo[0, j] = edge_out[j]
        first[j] = jnp.zeros((16, 128), F32)
        last[j] = jnp.zeros((16, 128), F32)

    def start(n, carry):
        for j in range(5):
            state[0, j, n + 1] = tall(full, 16 * j + n)
        return carry

    lax.fori_loop(0, LAYERS, start, 0)

    def store(i, n, value):
        out[i, n] = value

    for turn in range(SW):
        sweep(
            turn % 2, LAYERS, state, halo, first, last, rolled,
            coef_of(full), lambda i, n: tall(full, 80 + 16 * i + n),
            lambda k: edge_out[10 + k], lambda i: edge_out[5 + i],
            upwind, downwind, store if turn == SW - 1 else None,
        )


def final_kernel(
    span, prow, upwind, downwind, base, full, edges, across, r1, r2, r3, inside, shell, part,
    out, shell_out, reach, state, halo, first, last, rolled,
):
    shell_out[...] = shell[...]
    shell_out[:, 0:128] = shell[:, 0:128] + part[24:30, :]
    even = span[0] % 2 == 0
    x, y = across[...], inside[...]
    blocks = (jnp.where(even, x, y), r1[...], r2[...], r3[...], jnp.where(even, y, x))
    for b, value in enumerate(blocks):
        for i in range(3):
            reach[40 * i + 8 * b : 40 * i + 8 * b + 8, :] = value[8 * i : 8 * i + 8]
    walls = edges[FIELDS - 1]
    wall_planes = [pltpu.roll(walls, 128 - 8 * i, 1) if i else walls for i in range(4)]
    lane = iota((16, 128), 1)
    few = iota((8, 128), 1) < 8
    packed = jnp.where(few, wall_planes[3][0:8], pltpu.roll(wall_planes[3][8:16], 8, 1))
    base_node = (span[0] - 2) * NODE_DEV
    index = [v.astype(jnp.int32) - base_node for v in (full[227], full[PLANES + 227], packed)]
    tiles, lows = [v >> 7 for v in index], [v & 127 for v in index]

    def pick(h, got, wanted):
        got = list(got)
        for i in range(3):
            row = jnp.broadcast_to(reach[pl.ds(40 * i + h, 1), :], (8, 128))
            for q in wanted:
                value = jnp.take_along_axis(row, lows[q], axis=1)
                got[3 * i + q] = jnp.where(tiles[q] == h, value, got[3 * i + q])
        return tuple(got)

    got = tuple(jnp.zeros((8, 128), F32) for _ in range(9))
    outer, inner = functools.partial(pick, wanted=(1, 2)), functools.partial(pick, wanted=(0, 1, 2))
    got = lax.fori_loop(0, 8, outer, got, unroll=4)
    got = lax.fori_loop(8, 32, inner, got, unroll=4)
    got = lax.fori_loop(32, 40, outer, got, unroll=4)
    disp = sum(
        tall(full, 224 + i) * jnp.concatenate(got[3 * i : 3 * i + 2], axis=0) for i in range(3)
    )
    side = sum(
        wall_planes[i]
        * jnp.concatenate([got[3 * i + 2], pltpu.roll(got[3 * i + 2], 120, 1)], axis=0)
        for i in range(3)
    )
    side = jnp.where(lane < 8, side, 0.0)
    state[...] = jnp.zeros(state.shape, F32)
    for j in range(5):
        state[0, j, 1] = tall(full, 160) * (-prow[j] * disp)
        halo[0, j] = edges[10] * (-prow[j] * side)
        first[j] = jnp.zeros((16, 128), F32)
        last[j] = jnp.zeros((16, 128), F32)
    out[...] = base[...]

    def store(i, n, value):
        out[i, n] = base[i, n] + value

    for turn in range(1, SW):
        sweep(
            (turn + 1) % 2, turn + 1, state, halo, first, last, rolled,
            coef_of(full), lambda i, n: (-prow[i] * jnp.where(n == 0, 1.0, 0.0)) * disp,
            lambda k: edges[10 + k], lambda i: -prow[i] * side,
            upwind, downwind, store if turn == SW - 1 else None,
        )


def along_span(value, steps):
    count = lax.axis_size("span")
    first, last = max(0, -steps), min(count, count - steps)
    return lax.ppermute(value, "span", [(i, i + steps) for i in range(first, last)])


def exchange(to_upper, to_lower):
    even = lax.axis_index("span") % 2 == 0
    count = lax.axis_size("span")
    across = jnp.where(even, to_lower, to_upper)
    across = lax.ppermute(across, "span", cross_pairs(count))
    inside = jnp.where(even, to_upper, to_lower)
    inside = lax.ppermute(inside, "span", inside_pairs(count))
    return jnp.where(even, across, inside), jnp.where(even, inside, across)


def cross_pairs(count):
    return [(s, s - 1 + 2 * (s % 2)) for s in range(1, count - 1)]


def inside_pairs(count):
    return [(s, s ^ 1) for s in range(count)]


CHORD = ("far_z", "y")


def swap(value, bit):
    count = lax.axis_size(CHORD)
    return lax.ppermute(value, CHORD, [(c, c ^ bit) for c in range(count)])


def ring_parts(copies):
    return lax.all_to_all(copies, "y", 0, 0)


def per_device(
    adjoint_flow, flow_grad, diagonal, couplings, upwind, downwind, pressure_row, face_normal,
    face_node, face_count, adjoint_shell, shell_grad, node_precond, element_stiffness, connectivity,
):
    span = lax.axis_index("span").astype(jnp.int32).reshape(1)
    odd = (lax.axis_index("y") % 2).astype(jnp.int32).reshape(1)
    pack, rim, planes, to_inside, to_across, shell, sgrad, precond, walls = call(
        front_kernel,
        (
            sds(PACKED, 8, 128), sds(48, 128), sds(PLANES, 8, 128), sds(HALF, 8, 128),
            sds(HALF, 8, 128), sds(6, NODE_DEV), sds(6, NODE_DEV), sds(6, 6, NODE_DEV),
            sds(9, 8, 128),
        ),
        (
            span, face_count, adjoint_flow, flow_grad, diagonal, couplings, face_normal, face_node,
            element_stiffness, connectivity, adjoint_shell, shell_grad, node_precond,
        ),
        [SM] * 2 + [pl.BlockSpec(memory_space=pltpu.MemorySpace.HBM)] * 11,
        4 << 20,
        (
            pltpu.VMEM((LAYERS, 8, 128), F32), pltpu.VMEM((8, 128), jnp.int32),
            pltpu.VMEM((4, 128), jnp.int32), pltpu.SemaphoreType.DMA((32,)),
        ),
        vmem=60,
    )
    rim = along_span(rim, -1)
    spans = lax.axis_size("span")
    halo_across = lax.ppermute(to_across, "span", cross_pairs(spans))
    halo_inside = lax.ppermute(to_inside, "span", inside_pairs(spans))
    loads = call(
        load_kernel,
        sds(24, 8, 128),
        (span, pressure_row, walls),
        [SM] * 2 + [VM],
        4 << 20,
        (
            pltpu.VMEM((8, 1024), F32),
            pltpu.VMEM((8, 1024), jnp.int32),
            pltpu.VMEM((128, 1024), BF16),
        ),
    )
    apply_scratch = lambda nb: (
        pltpu.VMEM((8, 512 * nb), jnp.int32),
        pltpu.VMEM((128, 512 * nb), BF16),
        pltpu.VMEM((24, 128), F32),
        pltpu.VMEM((8, 512 * nb), F32),
    )
    own, inside, across, down2 = call(
        first_kernel,
        (sds(TILES, 8, 128), sds(TILES, 8, 128), sds(TILES, 8, 128), sds(8, 128)),
        (span, loads, shell, rim, pack),
        [SM] + [VM] * 4,
        4 << 20,
        apply_scratch(1),
    )
    across = lax.ppermute(across, "span", cross_pairs(spans))
    inside = lax.ppermute(inside, "span", inside_pairs(spans))
    even = span[0] % 2 == 0
    up, down = jnp.where(even, across, inside), jnp.where(even, inside, across)
    down2 = along_span(down2, -2)
    full, edges = call(
        pack_chord_kernel,
        (sds(SLOTS, 8, 128), sds(FIELDS, 16, 128)),
        (span, planes, halo_inside, halo_across),
        [SM] + [VM] * 3,
        4 << 20,
    )
    count = lax.axis_size(CHORD)
    pairs = [(c, c - 1 + 2 * (c % 2)) for c in range(1, count - 1)]
    far = lax.ppermute(edges, CHORD, pairs)
    near = swap(edges, 1)
    total = own + jnp.concatenate([up[:8] + down[:8], (down[8] + down2)[None]], axis=0)
    total = total.at[0].add(up[8])
    total = ring_parts(jnp.broadcast_to(total[None], (RING, *total.shape))).sum(0)
    scratch = lambda layers: (
        pltpu.VMEM((2, 5, layers + 2, 16, 128), F32),
        pltpu.VMEM((2, 5, 16, 128), F32),
        pltpu.VMEM((5, 16, 128), F32),
        pltpu.VMEM((5, 16, 128), F32),
        pltpu.VMEM((5, 4, 16, 128), F32),
    )
    remote = swap(jnp.concatenate([pack, total], axis=0), 4)
    base, edges = call(
        base_kernel,
        (sds(5, LAYERS, 8, 128), sds(FIELDS, 16, 128)),
        (odd, full, near, far, upwind, downwind),
        [SM] + [VM] * 3 + [SM] * 2,
        16 << 20,
        scratch(LAYERS),
    )
    pieces = (total, remote, sgrad, rim)
    res = sums = total
    lead = jnp.arange(128) < NB
    for turn in range(2):
        res, sums, force = call(
            functools.partial(step_kernel, turn == 0),
            (sds(TILES, 8, 128), sds(TILES, 8, 128), sds(RING, TILES, 8, 128)),
            (pack, remote if turn == 0 else far_pack, rim, precond, sums) + pieces,
            [VM] * (5 + len(pieces)),
            8 << 20,
            apply_scratch(2),
        )
        far_pack = remote if turn == 0 else far_pack
        force = ring_parts(force)
        pieces = (force, res)
        if turn == 0:
            pieces += exchange(force[:, 8].sum(0), jnp.where(lead, force[:, 0].sum(0), 0.0))
    shell, reach = call(
        last_kernel,
        (sds(6, NODE_DEV), sds(32, 128)),
        (shell, rim, precond, sums) + pieces,
        [VM] * (4 + len(pieces)),
        1 << 20,
    )
    lower = along_span(reach[24:], 2)
    below, above = exchange(reach, reach)
    mend = lambda value, part: (
        value[:24].reshape(3, 8, 128).at[:, 0].add(part[:3]).reshape(24, 128)
    )
    part = below
    reach, below, above = mend(reach, below[24:]), mend(below, lower), mend(above, reach[24:])
    even = span[0] % 2 == 0
    across = lax.ppermute(jnp.where(even, above, below), "span", cross_pairs(spans))
    inside = lax.ppermute(jnp.where(even, below, above), "span", inside_pairs(spans))
    reaches = (across, below, reach, above, inside, shell, part)
    flow, shell = call(
        final_kernel,
        (sds(5, LAYERS, 8, 128), sds(6, NODE_DEV)),
        (span, pressure_row, upwind, downwind, base, full, edges, *reaches),
        [SM] * 4 + [VM] * 10,
        8 << 20,
        (pltpu.VMEM((120, 128), F32), *scratch(SW)),
    )
    return flow, shell


def solution(mesh):
    spans, chords = mesh.devices.shape
    split = Mesh(mesh.devices.reshape(spans, 2, chords // 2), ("span", *CHORD))
    return jax.shard_map(
        per_device,
        mesh=split,
        in_specs=(
            P(None, None, "span", CHORD),
            P(None, None, "span", CHORD),
            P(None, "span", CHORD),
            P(None, None, "span", CHORD),
            P(),
            P(),
            P(),
            P(None, "span", CHORD),
            P("span", CHORD),
            P("span", CHORD),
            P(None, "span"),
            P(None, "span"),
            P(None, None, "span"),
            P(None, None, ("span", *CHORD)),
            P(None, ("span", *CHORD)),
        ),
        out_specs=(P(None, None, "span", CHORD), P(None, "span")),
        check_vma=False,
    )
```
